128 devices in a mesh: row: 32 (over x, z, core), col: 4 (over y).
Axes of the slice: x: 4, y: 4, z: 4, core: 2. Of those that a mesh axis runs over, the one named last changes fastest.
Arguments:
- subspace: bfloat16 [256, 131072], P('col', 'row'), may hold values from -400 to 400
- onsite: float32 [131072], P('row'), may hold values from -1.5 to 1.5
- blocks: bfloat16 [20, 1024, 128, 128], P(None, 'row'), may hold values from -0.125 to 0.125
- cols: int32 [1024, 20], replicated, may hold values from 0 to 1023, as said below
Outputs:
- basis: float32 [256, 131072], P('col', 'row')
- factor: float32 [256, 256], replicated
The draws below stay inside these ranges and needn't reach their ends.
Inputs may be any that keep to these rules, and one draw needn't show every extreme that they name: `cols`: the block rows are numbered by device: device r of row holds block rows r * 32 to (r + 1) * 32 - 1. A block row names block rows of its own device or of the devices r + 1, r - 1, r + 2 and r + 16 along row, counted round. The block rows of one device name between 1 and 4 distinct block rows of each of these four devices, and in every draw some device names exactly 4 on each of its four.
All inputs are finite; a program needn't handle non-finite values.
Results may differ from the reference program's by a relative error of at most 0.0044.
Values may be sent and summed in bfloat16 or wider, within the bound.
No kernel may reach another device: no remote copies, remote signals or barrier semaphores. Data moves between devices by JAX's collectives and lax.ppermute only.
A program may use at most 128 MiB of HBM per device.

```python
import math
import jax
import jax.numpy as jnp
from jax import lax

BS = 128
NNZ = 20
S = 256
HALO = 4
FILTER = 4
BR_DEV = 32
NB = 1024
NTOT = 131072


remote_slots = 4


def draw_cols(key, part):
    row_count = NB // BR_DEV
    keys = jax.random.split(jax.random.fold_in(key, 7), 5)
    counts = jax.random.randint(keys[0], (row_count, 4), 1, HALO + 1)
    busiest = jax.random.randint(keys[1], (), 0, row_count)
    counts = jnp.where(jnp.arange(row_count)[:, None] == busiest, HALO, counts)
    scores = jax.random.randint(keys[2], (row_count, 4, BR_DEV), 0, 2 ** 20) * BR_DEV + jnp.arange(BR_DEV)
    orders = jnp.argsort(scores, axis=-1).astype(jnp.int32)
    local_rows = jnp.arange(BR_DEV)[:, None]
    slot_ids = jnp.arange(NNZ)[None, :]
    pair_ids = (local_rows * remote_slots + slot_ids) % (4 * HALO)
    group_ids = pair_ids // HALO
    member_ids = pair_ids % HALO
    device_ids = jnp.arange(row_count)[:, None, None]
    valid = (slot_ids < remote_slots)[None] & (member_ids[None] < counts[device_ids, group_ids[None]])
    offsets = jnp.array([1, -1, 2, row_count // 2], dtype=jnp.int32)
    owners = (device_ids + offsets[group_ids][None]) % row_count
    chosen = orders[device_ids, group_ids[None], member_ids[None]]
    remote = owners * BR_DEV + chosen
    local = jax.random.randint(keys[3], (row_count, BR_DEV, NNZ), 0, BR_DEV) + device_ids * BR_DEV
    named = jnp.where(valid, remote, local)
    slot_scores = jax.random.randint(keys[4], (row_count, BR_DEV, NNZ), 0, 2 ** 20) * NNZ + jnp.arange(NNZ)
    slot_order = jnp.argsort(slot_scores, axis=-1)
    named = jnp.take_along_axis(named, slot_order, axis=-1)
    return named.reshape(NB, NNZ).astype(jnp.int32)


def draw_subspace(key, part):
    keys = jax.random.split(jax.random.fold_in(key, 11), 3)
    values = jax.random.normal(keys[0], (S, NTOT), jnp.float32)
    column_scale = jnp.exp(jax.random.uniform(keys[1], (S, 1), jnp.float32) * math.log(10.0))
    row_scale = jnp.exp(jax.random.uniform(keys[2], (1, NTOT), jnp.float32) * math.log(10.0))
    row_scale = row_scale * 3.0 ** (jnp.arange(NTOT, dtype=jnp.float32)[None, :] / NTOT)
    return (0.1 * values * column_scale * row_scale).astype(jnp.bfloat16)


def level_of(stream_key, dims, cuts, smallest, largest):
    def one(axis_at, blocks):
        draws = jax.random.uniform(jax.random.fold_in(jax.random.fold_in(stream_key, 6), axis_at), (blocks,), jnp.float32, smallest / len(cuts), largest / len(cuts))
        return jnp.repeat(jnp.exp(draws), dims[axis_at] // blocks).reshape((-1,) + (1,) * (len(dims) - axis_at - 1))

    loudness = one(*cuts[0])
    for cut in cuts[1:]:
        loudness = loudness * one(*cut)
    return loudness


def noise(key, extent, deviation, bound, cuts=(), kind=jnp.bfloat16):
    level = level_of(key, extent, cuts, -0.22, 0.18) if cuts else 1.0
    entries = jax.random.normal(key, extent, jnp.float32) * deviation * level
    return jnp.minimum(jnp.maximum(entries, -bound), bound).astype(kind)


def setup_inputs(seed: int = 0) -> dict:
    key_list = jax.random.split(jax.random.key(seed), 5)
    subspace = draw_subspace(jax.random.fold_in(key_list[4], 71), 0)
    onsite = jnp.clip(jax.random.uniform(key_list[1], (NTOT,), jnp.float32, -1.5, 1.5) * level_of(key_list[1], (NTOT,), ((0, 32),), -0.4, 0.0), -1.5, 1.5)
    blocks = noise(key_list[2], (NNZ, NB, BS, BS), (NNZ * BS) ** -0.5, 0.125, ((1, 32),))
    cols = draw_cols(jax.random.fold_in(key_list[4], 71), 0)
    return {"subspace": subspace, "onsite": onsite, "blocks": blocks, "cols": cols}


filter_scale = 0.4

def couple(lowered, onsite, blocks, cols):
    shaped = lowered.reshape(S, NB, BS)

    def add_slot(total, pair):
        slot_cols, slot_blocks = pair
        taken = jnp.take(shaped, slot_cols, axis=1).astype(jnp.float32)
        return (total + jnp.einsum('cla,lab->clb', taken, slot_blocks.astype(jnp.float32)), None)
    total, _ = lax.scan(add_slot, jnp.zeros((S, NB, BS), jnp.float32), (cols.T, blocks))
    return total.reshape(S, NTOT) + onsite[None, :] * lowered.astype(jnp.float32)

def reference(subspace, onsite, blocks, cols):
    previous = subspace.astype(jnp.float32)
    current = filter_scale * couple(subspace, onsite, blocks, cols)
    for filter_step in range(FILTER - 1):
        lowered = current.astype(jnp.bfloat16)
        following = 2.0 * filter_scale * couple(lowered, onsite, blocks, cols) - previous
        previous, current = (current, following)
    final = current.astype(jnp.bfloat16)
    gram = jnp.dot(final.astype(jnp.float32), final.T.astype(jnp.float32), preferred_element_type=jnp.float32)
    lower = jnp.linalg.cholesky(gram)
    inverse = lax.linalg.triangular_solve(lower, jnp.eye(S, dtype=jnp.float32), left_side=True, lower=True)
    basis = math.sqrt(NTOT) * jnp.dot(inverse, final.astype(jnp.float32), precision=lax.Precision.HIGHEST)
    factor = lower.T / math.sqrt(NTOT)
    return (basis, factor)
```

```python
import functools
import math

import jax
import jax.numpy as jnp
from jax import lax
from jax.experimental import pallas as pl
from jax.experimental.pallas import tpu as pltpu
from jax.sharding import PartitionSpec as P

HALO = 4
FILTER = 4
ROWS = 2
CHUNK = 8
RING = 16

filter_scale = 0.4


def offsets(row_count):
    return (1, -1, 2, row_count // 2)


def ranks_of(hits):
    return jnp.cumsum(hits.astype(jnp.int32), axis=-1) - 1


def plan(cols, row_index, row_count, local_blocks):
    slot_count = cols.shape[1]
    slots = local_blocks * slot_count
    by_device = cols.reshape(row_count, slots)
    deltas = jnp.array(offsets(row_count), jnp.int32)
    local_ids = jnp.arange(local_blocks, dtype=jnp.int32)
    own = lax.dynamic_index_in_dim(by_device, row_index, 0, keepdims=False)
    askers = (row_index - deltas) % row_count
    asked = jnp.take(by_device, askers, axis=0) - row_index * local_blocks
    asked_hits = jnp.any(asked[:, :, None] == local_ids, axis=1)
    asked_ranks = ranks_of(asked_hits)
    wanted = jnp.arange(HALO, dtype=jnp.int32)
    pick = asked_hits[:, None, :] & (asked_ranks[:, None, :] == wanted[None, :, None])
    send = jnp.sum(jnp.where(pick, local_ids, 0), axis=-1).reshape(-1)
    sources = (row_index + deltas) % row_count
    named_ids = (sources[:, None] * local_blocks + local_ids).reshape(-1)
    matches = own[:, None] == named_ids
    named_hits = jnp.any(matches, axis=0).reshape(len(deltas), local_blocks)
    base = HALO * jnp.arange(len(deltas), dtype=jnp.int32)
    places = (ranks_of(named_hits) + base[:, None]).reshape(-1)
    slot_place = jnp.sum(jnp.where(matches, places, 0), axis=-1)
    within = own - row_index * local_blocks
    is_local = (within >= 0) & (within < local_blocks)
    position = jnp.where(is_local, within, local_blocks)
    order = ranks_of(~is_local)
    slot_ids = jnp.arange(slots, dtype=jnp.int32)
    hit = (~is_local)[:, None] & (order[:, None] == slot_ids)
    code = slot_ids * 32 + slot_place
    pad_code = HALO * len(deltas)
    listed = jnp.sum(jnp.where(hit, code[:, None] - pad_code, 0), axis=0) + pad_code
    count = (order[-1:] + 1).astype(jnp.int32)
    return position, jnp.concatenate([count, send, listed])


def local_kernel(scale, first, pos, *refs):
    if first:
        blocks, x, onsite, y, held = refs
    else:
        blocks, x, onsite, prev, y, held = refs
    step = pl.program_id(0)
    slot_count, rows, size, _ = blocks.shape
    local_blocks = held.shape[0] - 1

    @pl.when(step == 0)
    def _():
        for j in range(local_blocks):
            held[j] = x[:, j * size : (j + 1) * size]
        held[local_blocks] = jnp.zeros(held.shape[1:], held.dtype)

    for r in range(rows):
        row = step * rows + r
        taken = jnp.concatenate(
            [held[pos[row * slot_count + s]] for s in range(slot_count)], axis=1
        )
        product = jnp.dot(
            taken,
            blocks[:, r].reshape(slot_count * size, size),
            preferred_element_type=jnp.float32,
        )
        span = slice(r * size, (r + 1) * size)
        value = scale * (product + onsite[:, span] * held[row].astype(jnp.float32))
        y[:, span] = value if first else value - prev[:, span]


def local_part(scale, pos, blocks, x, onsite, prev):
    slot_count, local_blocks, size, _ = blocks.shape
    width = x.shape[0]
    first = prev is None
    wide = ROWS * size
    in_specs = [
        pl.BlockSpec((slot_count, ROWS, size, size), lambda g, p: (0, g, 0, 0)),
        pl.BlockSpec(x.shape, lambda g, p: (0, 0)),
        pl.BlockSpec((1, wide), lambda g, p: (0, g)),
    ]
    args = [blocks, x, onsite]
    if not first:
        in_specs.append(pl.BlockSpec((width, wide), lambda g, p: (0, g)))
        args.append(prev)
    return pl.pallas_call(
        functools.partial(local_kernel, scale, first),
        out_shape=jax.ShapeDtypeStruct(x.shape, jnp.float32),
        grid_spec=pltpu.PrefetchScalarGridSpec(
            num_scalar_prefetch=1,
            grid=(local_blocks // ROWS,),
            in_specs=in_specs,
            out_specs=pl.BlockSpec((width, wide), lambda g, p: (0, g)),
            scratch_shapes=[pltpu.VMEM((local_blocks + 1, width, size), jnp.bfloat16)],
        ),
        name="local_part",
    )(pos, *args)


def remote_kernel(scale, last, info, *refs):
    halos, rest = refs[:4], refs[4:]
    y_in, blocks, y, x, send, zero, held, sems = rest
    slot_count, local_blocks, size, _ = blocks.shape
    per = halos[0].shape[0]
    count = info[0]
    list_at = 1 + 4 * per
    chunks = (count + CHUNK - 1) // CHUNK

    def start(c):
        slot = lax.rem(c, RING)
        for k in range(CHUNK):
            entry = info[list_at + c * CHUNK + k] // 32
            row = entry // slot_count
            pltpu.make_async_copy(
                blocks.at[entry - row * slot_count, row],
                held.at[slot * CHUNK + k],
                sems.at[slot],
            ).start()

    @pl.loop(0, jnp.minimum(chunks, RING))
    def _(c):
        start(c)

    for q in range(4):
        zero[q * per : (q + 1) * per] = halos[q][...]
    zero[4 * per] = jnp.zeros(zero.shape[1:], zero.dtype)
    y[...] = y_in[...]

    @pl.loop(0, chunks)
    def _(c):
        slot = lax.rem(c, RING)
        part = held.at[pl.ds(slot * CHUNK, CHUNK)]
        pltpu.make_async_copy(part, part, sems.at[slot]).wait()
        for k in range(CHUNK):
            code = info[list_at + c * CHUNK + k]
            entry = code // 32
            place = lax.rem(code, 32)
            row = entry // slot_count
            product = jnp.dot(
                zero[place], held[slot * CHUNK + k], preferred_element_type=jnp.float32
            )
            span = pl.ds(pl.multiple_of(row * size, size), size)
            y[:, span] = y[:, span] + scale * product

        @pl.when(c + RING < chunks)
        def _():
            start(c + RING)

    x[...] = y[...].astype(jnp.bfloat16)
    if not last:
        for q in range(4):
            for k in range(per):
                j = info[1 + q * per + k]
                send[q, k] = x[:, pl.ds(pl.multiple_of(j * size, size), size)]
    else:
        own = info[list_at + slot_count * local_blocks]
        piece = x.shape[1] // 4
        for k in range(1, 4):
            at = lax.rem(own + k, 4) * piece
            send[k - 1] = x[:, pl.ds(pl.multiple_of(at, piece), piece)]


def remote_part(scale, last, info, halos, y, blocks):
    slot_count, local_blocks, size, _ = blocks.shape
    width, local_rows = y.shape
    per = halos[0].shape[0]
    vmem = pl.BlockSpec(memory_space=pltpu.VMEM)
    if last:
        send = (3, width, local_rows // 4)
    else:
        send = (4, per, width, size)
    return pl.pallas_call(
        functools.partial(remote_kernel, scale, last),
        out_shape=(
            jax.ShapeDtypeStruct(y.shape, jnp.float32),
            jax.ShapeDtypeStruct(y.shape, jnp.bfloat16),
            jax.ShapeDtypeStruct(send, jnp.bfloat16),
        ),
        in_specs=[pl.BlockSpec(memory_space=pltpu.SMEM)]
        + [vmem] * 5
        + [pl.BlockSpec(memory_space=pl.ANY)],
        out_specs=(vmem,) * 3,
        scratch_shapes=[
            pltpu.VMEM((4 * per + 1, width, size), jnp.bfloat16),
            pltpu.VMEM((RING * CHUNK, size, size), jnp.bfloat16),
            pltpu.SemaphoreType.DMA((RING,)),
        ],
        name="remote_part",
    )(info, *halos, y, blocks)


def shift(value, axis, by):
    n = lax.axis_size(axis)
    return lax.ppermute(value, axis, [(i, (i + by) % n) for i in range(n)])


def swap(value, axis, mask):
    n = lax.axis_size(axis)
    return lax.ppermute(value, axis, [(i, i ^ mask) for i in range(n)])


def xor_sum(value, axis, masks):
    terms = [value] + [swap(value, axis, m) for m in masks]
    while len(terms) > 1:
        terms = [terms[i] + terms[i + 1] for i in range(0, len(terms), 2)]
    return terms[0]


def body(subspace, onsite, blocks, cols):
    row_count = lax.axis_size("row")
    row_index = lax.axis_index("row")
    col_count = lax.axis_size("col")
    col_index = lax.axis_index("col")
    width, local_rows = subspace.shape
    slot_count, local_blocks, size, _ = blocks.shape
    total_cols = width * col_count
    pos, info = plan(cols, row_index, row_count, local_blocks)
    info = jnp.concatenate([info, col_index[None].astype(jnp.int32)])
    onsite = onsite[None, :]
    shaped = subspace.reshape(width, local_blocks, size)
    chosen = jnp.take(shaped, info[1 : 1 + 4 * HALO], axis=1)
    send = chosen.transpose(1, 0, 2).reshape(4, HALO, width, size)
    previous, x = None, subspace
    before = subspace.astype(jnp.float32)
    for step in range(FILTER):
        scale = filter_scale if step == 0 else 2.0 * filter_scale
        last = step == FILTER - 1
        halos = [shift(send[q], "row", -d) for q, d in enumerate(offsets(row_count))]
        partial = local_part(scale, pos, blocks, x, onsite, previous)
        y, x, send = remote_part(scale, last, info, halos, partial, blocks)
        previous, before = before, y
    final = x
    piece = local_rows // col_count
    mine = lax.dynamic_slice_in_dim(final, col_index * piece, piece, 1)
    got = [shift(send[k - 1], "col", k) for k in range(1, col_count)]
    others = [shift(final, "col", k) for k in range(1, col_count)]
    stack = jnp.concatenate([mine] + got, axis=0)
    gram = jnp.einsum("ar,br->ab", stack, stack, preferred_element_type=jnp.float32)
    gram = gram.reshape(col_count, width, col_count, width)
    order = (col_index - jnp.arange(col_count)) % col_count
    gram = jnp.take(jnp.take(gram, order, axis=0), order, axis=2)
    gram = gram.reshape(col_count, width, total_cols)

    def part(k):
        return lax.dynamic_index_in_dim(gram, (col_index + k) % col_count, 0, keepdims=False)

    strip = part(0)
    for k in range(1, col_count):
        strip = strip + shift(part(k), "col", k)
    low = row_count // 4
    strip = xor_sum(strip, "row", list(range(1, low)))
    strip = xor_sum(strip, "row", [low * m for m in (1, 2, 3)])
    strips = jnp.stack([strip] + [shift(strip, "col", k) for k in range(1, col_count)])
    gram = jnp.take(strips, order, axis=0).reshape(total_cols, total_cols)
    lower = jnp.linalg.cholesky(gram)
    total_rows = row_count * local_rows
    inverse = lax.linalg.triangular_solve(
        lower, jnp.eye(total_cols, dtype=jnp.float32), left_side=True, lower=True
    )
    own_part = lax.dynamic_slice_in_dim(inverse, col_index * width, width, 0)
    own_part = own_part.reshape(width, col_count, width)
    own_part = jnp.take(own_part, order, axis=1).reshape(width, total_cols)
    whole = jnp.concatenate([final] + others, axis=0)
    basis = math.sqrt(total_rows) * jnp.dot(
        own_part, whole.astype(jnp.float32), precision=lax.Precision.HIGHEST
    )
    factor = lower.T / math.sqrt(total_rows)
    return (basis, factor)


def solution(mesh):
    in_specs = (P("col", "row"), P("row"), P(None, "row", None, None), P())
    out_specs = (P("col", "row"), P())
    return jax.shard_map(body, mesh=mesh, in_specs=in_specs, out_specs=out_specs, check_vma=False)
```

```python
import functools
import math

import jax
import jax.numpy as jnp
from jax import lax
from jax.experimental import pallas as pl
from jax.experimental.pallas import tpu as pltpu
from jax.sharding import PartitionSpec as P

HALO = 4
FILTER = 4
UNROLL = 4
CHUNK = 8
PANEL = 16

filter_scale = 0.4


def offsets(row_count):
    return (1, -1, 2, row_count // 2)


def ranks_of(hits):
    return jnp.cumsum(hits.astype(jnp.int32), axis=-1) - 1


def plan(cols, row_index, row_count, local_blocks):
    slot_count = cols.shape[1]
    slots = local_blocks * slot_count
    by_device = cols.reshape(row_count, slots)
    deltas = jnp.array(offsets(row_count), jnp.int32)
    local_ids = jnp.arange(local_blocks, dtype=jnp.int32)
    own = lax.dynamic_index_in_dim(by_device, row_index, 0, keepdims=False)
    askers = (row_index - deltas) % row_count
    asked = jnp.take(by_device, askers, axis=0) - row_index * local_blocks
    asked_hits = jnp.any(asked[:, :, None] == local_ids, axis=1)
    asked_ranks = ranks_of(asked_hits)
    wanted = jnp.arange(HALO, dtype=jnp.int32)
    pick = asked_hits[:, None, :] & (asked_ranks[:, None, :] == wanted[None, :, None])
    send = jnp.sum(jnp.where(pick, local_ids, 0), axis=-1).reshape(-1)
    sources = (row_index + deltas) % row_count
    named_ids = (sources[:, None] * local_blocks + local_ids).reshape(-1)
    matches = own[:, None] == named_ids
    named_hits = jnp.any(matches, axis=0).reshape(len(deltas), local_blocks)
    base = HALO * jnp.arange(len(deltas), dtype=jnp.int32)
    places = (ranks_of(named_hits) + base[:, None]).reshape(-1)
    slot_place = jnp.sum(jnp.where(matches, places, 0), axis=-1)
    within = own - row_index * local_blocks
    is_local = (within >= 0) & (within < local_blocks)
    position = jnp.where(is_local, within, local_blocks)
    order = ranks_of(~is_local)
    slot_ids = jnp.arange(slots, dtype=jnp.int32)
    hit = (~is_local)[:, None] & (order[:, None] == slot_ids)
    code = slot_ids * 32 + slot_place
    pad_code = HALO * len(deltas)
    listed = jnp.sum(jnp.where(hit, code[:, None] - pad_code, 0), axis=0) + pad_code
    count = (order[-1:] + 1).astype(jnp.int32)
    return position, jnp.concatenate([count, send, listed])


def local_kernel(scale, first, pos, blocks, x, onsite, *refs):
    prev, y, held = (None, *refs) if first else refs
    slot_count, local_blocks, size, _ = blocks.shape
    for j in range(local_blocks):
        held[j] = x[:, j * size : (j + 1) * size]
    held[local_blocks] = jnp.zeros(held.shape[1:], held.dtype)

    @pl.loop(0, local_blocks // UNROLL)
    def _(group):
        for u in range(UNROLL):
            row = group * UNROLL + u
            total = None
            for s in range(0, slot_count, 2):
                at = row * slot_count + s
                taken = jnp.concatenate([held[pos[at]], held[pos[at + 1]]], axis=1)
                block = jnp.concatenate([blocks[s, row], blocks[s + 1, row]], axis=0)
                product = jnp.dot(taken, block, preferred_element_type=jnp.float32)
                total = product if total is None else total + product
            span = pl.ds(pl.multiple_of(row * size, size), size)
            value = scale * (total + onsite[:, span] * held[row].astype(jnp.float32))
            if prev is not None:
                value = value - prev[:, span].astype(jnp.float32)
            y[:, span] = value


def remote_kernel(scale, last, info, *refs):
    halos, (y_in, blocks, y, x), rest = refs[:4], refs[4:8], refs[8:]
    sends, zero = rest[:-1], rest[-1]
    slot_count, local_blocks, size, _ = blocks.shape
    per = halos[0].shape[0]
    count = info[0]
    list_at = 1 + 4 * per
    for q in range(4):
        zero[q * per : (q + 1) * per] = halos[q][...]
    zero[4 * per] = jnp.zeros(zero.shape[1:], zero.dtype)
    y[...] = y_in[...]

    @pl.loop(0, (count + CHUNK - 1) // CHUNK)
    def _(c):
        for k in range(CHUNK):
            code = info[list_at + c * CHUNK + k]
            entry = code // 32
            place = lax.rem(code, 32)
            row = entry // slot_count
            slot = entry - row * slot_count
            product = jnp.dot(zero[place], blocks[slot, row], preferred_element_type=jnp.float32)
            span = pl.ds(pl.multiple_of(row * size, size), size)
            y[:, span] = y[:, span] + scale * product

    x[...] = y[...].astype(jnp.bfloat16)
    if not last:
        for q in range(4):
            for k in range(per):
                j = info[1 + q * per + k]
                sends[q][k] = x[:, pl.ds(pl.multiple_of(j * size, size), size)]
    else:
        own = info[list_at + slot_count * local_blocks]
        piece = x.shape[1] // 4
        for k in range(4):
            at = lax.rem(own + k, 4) * piece
            sends[k][...] = x[:, pl.ds(pl.multiple_of(at, piece), piece)]


vmem = pl.BlockSpec(memory_space=pltpu.VMEM)
smem = pl.BlockSpec(memory_space=pltpu.SMEM)
grant = pltpu.CompilerParams(vmem_limit_bytes=16 << 20)


def local_part(scale, pos, blocks, x, onsite, prev):
    _, local_blocks, size, _ = blocks.shape
    args = [pos, blocks, x, onsite] + ([] if prev is None else [prev])
    return pl.pallas_call(
        functools.partial(local_kernel, scale, prev is None),
        out_shape=jax.ShapeDtypeStruct(x.shape, jnp.float32),
        in_specs=[smem] + [vmem] * (len(args) - 1),
        out_specs=vmem,
        scratch_shapes=[pltpu.VMEM((local_blocks + 1, x.shape[0], size), jnp.bfloat16)],
        compiler_params=grant,
        name="local_part",
    )(*args)


def remote_part(scale, last, info, halos, y, blocks):
    size = blocks.shape[2]
    width, local_rows = y.shape
    per = halos[0].shape[0]
    send = (width, local_rows // 4) if last else (per, width, size)
    return pl.pallas_call(
        functools.partial(remote_kernel, scale, last),
        out_shape=(
            jax.ShapeDtypeStruct(y.shape, jnp.float32),
            jax.ShapeDtypeStruct(y.shape, jnp.bfloat16),
        )
        + (jax.ShapeDtypeStruct(send, jnp.bfloat16),) * 4,
        in_specs=[smem] + [vmem] * 6,
        out_specs=(vmem,) * 6,
        scratch_shapes=[pltpu.VMEM((4 * per + 1, width, size), jnp.bfloat16)],
        compiler_params=grant,
        name="remote_part",
    )(info, *halos, y, blocks)


def gram_kernel(*refs):
    pieces, strips = refs[:4], refs[4:]
    stack = jnp.concatenate([p[...] for p in pieces], axis=0)
    gram = lax.dot_general(
        stack, stack, (((1,), (1,)), ((), ())), preferred_element_type=jnp.float32
    )
    width = pieces[0].shape[0]
    for k in range(4):
        at = (-k) % 4 * width
        rows = gram[at : at + width]
        order = [(j - k) % 4 * width for j in range(4)]
        strips[k][...] = jnp.concatenate([rows[:, o : o + width] for o in order], axis=1)


def gram_strips(pieces):
    width = pieces[0].shape[0]
    return pl.pallas_call(
        gram_kernel,
        out_shape=(jax.ShapeDtypeStruct((width, 4 * width), jnp.float32),) * 4,
        in_specs=[vmem] * 4,
        out_specs=(vmem,) * 4,
        compiler_params=grant,
        name="gram_strips",
    )(*pieces)


def three_parts(value):
    high = value.astype(jnp.bfloat16)
    rest = value - high.astype(jnp.float32)
    middle = rest.astype(jnp.bfloat16)
    low = (rest - middle.astype(jnp.float32)).astype(jnp.bfloat16)
    return high, middle, low


def solve_kernel(root, own_ref, *refs):
    strips, finals, (basis, factor, work, inverse) = refs[:4], refs[4:8], refs[8:]
    own = own_ref[0]
    width, n = strips[0].shape
    f32 = jnp.float32
    for k in range(4):
        at = pl.multiple_of(lax.rem(own + 4 - k, 4) * width, width)
        work[pl.ds(at, width), :] = strips[k][...]
    row_ids = lax.broadcasted_iota(jnp.int32, (PANEL, 128), 0)
    lane_ids = lax.broadcasted_iota(jnp.int32, (PANEL, 128), 1)
    for r0 in range(0, n, PANEL):
        r1 = r0 + PANEL
        at, tile = r0 % 128, r0 // 128
        rows = work[r0:r1, :]
        pivots = [
            jnp.broadcast_to(rows[:, r0 + k : r0 + k + 1], (PANEL, 128)) for k in range(PANEL)
        ]
        parts = [rows[:, t : t + 128] for t in range(0, n, 128)]
        parts.append(jnp.where(lane_ids - at == row_ids, 1.0, 0.0).astype(f32))
        diagonal = jnp.ones((PANEL, 128), f32)
        for j in range(PANEL):
            pivot = pivots[j][j : j + 1, :]
            diagonal = jnp.where(row_ids == j, pivot, diagonal)
            factors = jnp.where(row_ids > j, pivots[j] * (1.0 / pivot), 0.0)
            for k in range(j + 1, PANEL):
                pivots[k] = pivots[k] - factors * pivots[k][j : j + 1, :]
            parts = [q - factors * q[j : j + 1, :] for q in parts]
        roots = lax.rsqrt(diagonal)
        parts = [q * roots for q in parts]
        in_panel = (lane_ids >= at) & (lane_ids < at + PANEL)
        joined = []
        for t in range(n // 128):
            cols = lane_ids + 128 * t
            span = slice(128 * t, 128 * t + 128)
            factor[r0:r1, span] = jnp.where(cols >= row_ids + r0, parts[t] * (1.0 / root), 0.0)
            both = jnp.where(in_panel, parts[-1], parts[t]) if t == tile else parts[t]
            joined.append(both)
            inverse[r0:r1, span] = jnp.where(cols < r1, both, 0.0)
        if r1 < n:
            h, m, l = three_parts(jnp.concatenate(joined, axis=1))
            left = jnp.concatenate([h, h, m, m, h, l], axis=0)
            right = jnp.concatenate([h, m, h, m, l, h], axis=0)
            low = r1 // 128 * 128
            update = lax.dot_general(
                left[:, low:], right, (((0,), (0,)), ((), ())), preferred_element_type=f32
            )
            cols = lax.broadcasted_iota(jnp.int32, (n - r1, n), 1)
            kept = jnp.where((cols >= r0) & (cols < r1), 0.0, work[r1:, :])
            work[r1:, :] = kept - update[r1 - low :, :]
    mine = root * inverse[pl.ds(pl.multiple_of(own * width, width), width), :]
    blocks = [mine[:, b * width : (b + 1) * width] for b in range(4)]
    ordered = []
    for k in range(4):
        source = lax.rem(own + 4 - k, 4)
        block = blocks[0]
        for b in range(1, 4):
            block = jnp.where(source == b, blocks[b], block)
        ordered.append(block)
    ordered = jnp.concatenate(ordered, axis=1)
    left = jnp.concatenate(three_parts(ordered), axis=0)
    wide = 512
    for c in range(0, basis.shape[1], wide):
        right = jnp.concatenate([f[:, c : c + wide] for f in finals], axis=0)
        product = jnp.dot(left, right, preferred_element_type=f32)
        basis[:, c : c + wide] = (
            product[:width] + product[width : 2 * width] + product[2 * width :]
        )


def solve(root, own, strips, finals):
    n = strips[0].shape[1]
    return pl.pallas_call(
        functools.partial(solve_kernel, root),
        out_shape=(
            jax.ShapeDtypeStruct(finals[0].shape, jnp.float32),
            jax.ShapeDtypeStruct((n, n), jnp.float32),
        ),
        in_specs=[smem] + [vmem] * 8,
        out_specs=(vmem,) * 2,
        scratch_shapes=[pltpu.VMEM((n, n), jnp.float32)] * 2,
        compiler_params=grant,
        name="solve",
    )(own, *strips, *finals)


def shift(value, axis, by):
    n = lax.axis_size(axis)
    return lax.ppermute(value, axis, [(i, (i + by) % n) for i in range(n)])


def swap(value, axis, mask):
    n = lax.axis_size(axis)
    return lax.ppermute(value, axis, [(i, i ^ mask) for i in range(n)])


def xor_sum(value, axis, masks):
    terms = [value] + [swap(value, axis, m) for m in masks]
    while len(terms) > 1:
        terms = [terms[i] + terms[i + 1] for i in range(0, len(terms), 2)]
    return terms[0]


def body(subspace, onsite, blocks, cols):
    row_count = lax.axis_size("row")
    row_index = lax.axis_index("row")
    col_index = lax.axis_index("col").astype(jnp.int32)
    width, local_rows = subspace.shape
    slot_count, local_blocks, size, _ = blocks.shape
    pos, info = plan(cols, row_index, row_count, local_blocks)
    info = jnp.concatenate([info, col_index[None]])
    onsite = onsite[None, :]
    shaped = subspace.reshape(width, local_blocks, size)
    chosen = jnp.take(shaped, info[1 : 1 + 4 * HALO], axis=1)
    send = chosen.transpose(1, 0, 2).reshape(4, HALO, width, size)
    previous, before, x = None, subspace, subspace
    for step in range(FILTER):
        scale = filter_scale if step == 0 else 2.0 * filter_scale
        last = step == FILTER - 1
        halos = [shift(send[q], "row", -d) for q, d in enumerate(offsets(row_count))]
        partial = local_part(scale, pos, blocks, x, onsite, previous)
        y, x, *send = remote_part(scale, last, info, halos, partial, blocks)
        previous, before = before, y
    final = x
    pieces = [send[0]] + [shift(send[k], "col", k) for k in (1, 2, 3)]
    strips = gram_strips(pieces)
    finals = [final] + [shift(final, "col", k) for k in (1, 2, 3)]
    strip = strips[0]
    for k in (1, 2, 3):
        strip = strip + shift(strips[k], "col", k)
    low = row_count // 4
    strip = xor_sum(strip, "row", list(range(1, low)))
    strip = xor_sum(strip, "row", [low * m for m in (1, 2, 3)])
    blocks_of = [strip[:, j * width : (j + 1) * width] for j in range(4)]
    ordered = []
    for b in range(4):
        j = (col_index - b) % 4
        ordered.append(
            jnp.where(
                j < 2,
                jnp.where(j == 0, blocks_of[0], blocks_of[1]),
                jnp.where(j == 2, blocks_of[2], blocks_of[3]),
            )
        )
    strip = jnp.concatenate(ordered, axis=1)
    strips = [strip] + [shift(strip, "col", k) for k in (1, 2, 3)]
    root = math.sqrt(row_count * local_rows)
    return solve(root, col_index[None], strips, finals)


def solution(mesh):
    in_specs = (P("col", "row"), P("row"), P(None, "row", None, None), P())
    out_specs = (P("col", "row"), P())
    return jax.shard_map(body, mesh=mesh, in_specs=in_specs, out_specs=out_specs, check_vma=False)
```

```python
import functools
import math

import jax
import jax.numpy as jnp
from jax import lax
from jax.experimental import pallas as pl
from jax.experimental.pallas import tpu as pltpu
from jax.sharding import PartitionSpec as P

HALO = 4
FILTER = 4
UNROLL = 4
LATE = 4
PANEL = 16

filter_scale = 0.4


def offsets(row_count):
    return (1, -1, 2, row_count // 2)


def ranks_of(hits):
    return jnp.cumsum(hits.astype(jnp.int32), axis=-1) - 1


def plan(cols, row_index, row_count, local_blocks):
    slot_count = cols.shape[1]
    slots = local_blocks * slot_count
    by_device = cols.reshape(row_count, slots)
    deltas = jnp.array(offsets(row_count), jnp.int32)
    local_ids = jnp.arange(local_blocks, dtype=jnp.int32)
    own = lax.dynamic_index_in_dim(by_device, row_index, 0, keepdims=False)
    askers = (row_index - deltas) % row_count
    asked = jnp.take(by_device, askers, axis=0) - row_index * local_blocks
    asked_hits = jnp.any(asked[:, :, None] == local_ids, axis=1)
    asked_ranks = ranks_of(asked_hits)
    wanted = jnp.arange(HALO, dtype=jnp.int32)
    pick = asked_hits[:, None, :] & (asked_ranks[:, None, :] == wanted[None, :, None])
    send = jnp.sum(jnp.where(pick, local_ids, 0), axis=-1).reshape(-1)
    sources = (row_index + deltas) % row_count
    named_ids = (sources[:, None] * local_blocks + local_ids).reshape(-1)
    matches = own[:, None] == named_ids
    named_hits = jnp.any(matches, axis=0).reshape(len(deltas), local_blocks)
    base = HALO * jnp.arange(len(deltas), dtype=jnp.int32)
    places = (ranks_of(named_hits) + base[:, None]).reshape(-1)
    slot_place = jnp.sum(jnp.where(matches, places, 0), axis=-1)
    within = own - row_index * local_blocks
    is_local = (within >= 0) & (within < local_blocks)
    place = jnp.where(is_local, within, local_blocks + 1 + slot_place)
    near = is_local.reshape(local_blocks, slot_count)
    near_rank = ranks_of(near)
    far_rank = near_rank[:, -1:] + 1 + ranks_of(~near)
    rank = jnp.where(near, near_rank, far_rank)
    slot_ids = jnp.arange(slot_count, dtype=jnp.int32)
    code = slot_ids * 64 + place.reshape(local_blocks, slot_count)
    sorts = rank[:, :, None] == slot_ids
    table = jnp.sum(jnp.where(sorts, code[:, :, None], 0), axis=1)
    extra = (slot_ids < slot_count - LATE) & (table % 64 > local_blocks)
    extra_code = (local_ids[:, None] * 2048 + table).reshape(-1)
    order = jnp.where(extra.reshape(-1), ranks_of(extra.reshape(-1)), -1)
    hit = order[:, None] == jnp.arange(slots, dtype=jnp.int32)
    listed = jnp.sum(jnp.where(hit, extra_code[:, None], 0), axis=0)
    count = jnp.sum(extra.astype(jnp.int32)).reshape(1)
    return table.reshape(-1), jnp.concatenate([send, count, listed])


def slot_pairs(table, row, slots, held, blocks, limit):
    slot_count = blocks.shape[0]
    total = None
    for t in range(slots.start, slots.stop, 2):
        codes = [table[row * slot_count + t + k] for k in range(2)]
        places = [jnp.minimum(code & 63, limit) for code in codes]
        taken = jnp.concatenate([held[p] for p in places], axis=1)
        block = jnp.concatenate([blocks[code >> 6, row] for code in codes], axis=0)
        product = jnp.dot(taken, block, preferred_element_type=jnp.float32)
        total = product if total is None else total + product
    return total


def local_kernel(scale, first, table, blocks, x, onsite, *refs):
    prev, y, held = (None, *refs) if first else refs
    slot_count, local_blocks, size, _ = blocks.shape
    for j in range(local_blocks):
        held[j] = x[:, j * size : (j + 1) * size]
    held[local_blocks] = jnp.zeros(held.shape[1:], held.dtype)

    @pl.loop(0, local_blocks // UNROLL)
    def _(group):
        for u in range(UNROLL):
            row = group * UNROLL + u
            early = range(slot_count - LATE)
            total = slot_pairs(table, row, early, held, blocks, local_blocks)
            span = pl.ds(pl.multiple_of(row * size, size), size)
            value = scale * (total + onsite[:, span] * held[row].astype(jnp.float32))
            if prev is not None:
                value = value - prev[:, span].astype(jnp.float32)
            y[:, span] = value


def remote_kernel(scale, last, info, table, *refs):
    halos, (y_in, x_in, blocks, y, x), rest = refs[:4], refs[4:9], refs[9:]
    sends, held = rest[:-1], rest[-1]
    slot_count, local_blocks, size, _ = blocks.shape
    per = halos[0].shape[0]
    count = info[4 * per]
    for j in range(local_blocks):
        held[j] = x_in[:, j * size : (j + 1) * size]
    held[local_blocks] = jnp.zeros(held.shape[1:], held.dtype)
    for q in range(4):
        at = local_blocks + 1 + q * per
        held[at : at + per] = halos[q][...]

    @pl.loop(0, local_blocks // UNROLL)
    def _(group):
        for u in range(UNROLL):
            row = group * UNROLL + u
            late = range(slot_count - LATE, slot_count)
            total = slot_pairs(table, row, late, held, blocks, held.shape[0] - 1)
            span = pl.ds(pl.multiple_of(row * size, size), size)
            value = y_in[:, span] + scale * total
            y[:, span] = value
            x[:, span] = value.astype(jnp.bfloat16)

    @pl.loop(0, count)
    def _(k):
        code = info[4 * per + 1 + k]
        row = code >> 11
        slot = (code >> 6) & 31
        product = jnp.dot(held[code & 63], blocks[slot, row], preferred_element_type=jnp.float32)
        span = pl.ds(pl.multiple_of(row * size, size), size)
        y[:, span] = y[:, span] + scale * product

    @pl.when(count > 0)
    def _():
        x[...] = y[...].astype(jnp.bfloat16)

    if not last:
        for q in range(4):
            for k in range(per):
                j = info[q * per + k]
                sends[q][k] = x[:, pl.ds(pl.multiple_of(j * size, size), size)]


vmem = pl.BlockSpec(memory_space=pltpu.VMEM)
smem = pl.BlockSpec(memory_space=pltpu.SMEM)
grant = pltpu.CompilerParams(vmem_limit_bytes=16 << 20)


def local_part(scale, pos, blocks, x, onsite, prev):
    _, local_blocks, size, _ = blocks.shape
    args = [pos, blocks, x, onsite] + ([] if prev is None else [prev])
    return pl.pallas_call(
        functools.partial(local_kernel, scale, prev is None),
        out_shape=jax.ShapeDtypeStruct(x.shape, jnp.float32),
        in_specs=[smem] + [vmem] * (len(args) - 1),
        out_specs=vmem,
        scratch_shapes=[pltpu.VMEM((local_blocks + 1, x.shape[0], size), jnp.bfloat16)],
        compiler_params=grant,
        name="local_part",
    )(*args)


def remote_part(scale, last, info, table, halos, y, x, blocks):
    _, local_blocks, size, _ = blocks.shape
    width = y.shape[0]
    per = halos[0].shape[0]
    sends = () if last else (jax.ShapeDtypeStruct((per, width, size), jnp.bfloat16),) * 4
    return pl.pallas_call(
        functools.partial(remote_kernel, scale, last),
        out_shape=(
            jax.ShapeDtypeStruct(y.shape, jnp.float32),
            jax.ShapeDtypeStruct(y.shape, jnp.bfloat16),
        )
        + sends,
        in_specs=[smem] * 2 + [vmem] * 7,
        out_specs=(vmem,) * (2 + len(sends)),
        scratch_shapes=[pltpu.VMEM((local_blocks + 1 + 4 * per, width, size), jnp.bfloat16)],
        compiler_params=grant,
        name="remote_part",
    )(info, table, *halos, y, x, blocks)


def gram_kernel(own, one, *refs):
    halves, strip = refs[:-1], refs[-1]
    f32 = jnp.float32
    nt = (((1,), (1,)), ((), ()))
    width = own.shape[0]
    other = jnp.concatenate([own[...], one[...]], axis=0)
    strip[:width, :] = lax.dot_general(own[...], other, nt, preferred_element_type=f32)
    two = jnp.concatenate([h[...] for h in halves], axis=1)
    block = lax.dot_general(own[...], two, nt, preferred_element_type=f32)
    half = width // 2
    strip[width:, :] = jnp.concatenate([block[:half], block[half:]], axis=1)


def gram_strip(own, one, halves):
    width = own.shape[0]
    return pl.pallas_call(
        gram_kernel,
        out_shape=jax.ShapeDtypeStruct((width + width // 2, 2 * width), jnp.float32),
        in_specs=[vmem] * 4,
        out_specs=vmem,
        compiler_params=grant,
        name="gram_strip",
    )(own, one, *halves)


def three_parts(value):
    high = value.astype(jnp.bfloat16)
    rest = value - high.astype(jnp.float32)
    middle = rest.astype(jnp.bfloat16)
    low = (rest - middle.astype(jnp.float32)).astype(jnp.bfloat16)
    return high, middle, low


def solve_kernel(root, own_ref, *refs):
    strips, finals, (basis, factor, work, inverse) = refs[:4], refs[4:9], refs[9:]
    own = own_ref[0]
    n = work.shape[0]
    width = n // 4
    half = width // 2
    f32 = jnp.float32
    for k in range(4):
        row = lax.rem(own + 4 - k, 4)
        tail = strips[k][width:, :]
        blocks = [
            strips[k][:width, :width],
            strips[k][:width, width:],
            jnp.concatenate([tail[:, :width], tail[:, width:]], axis=0),
        ]
        for part in range(4):

            @pl.when(row == part)
            def _(part=part, blocks=blocks):
                at = slice(part * width, (part + 1) * width)
                work[at, at] = blocks[0]
                for j in (1, 2):
                    col = (part - j) % 4
                    to = slice(col * width, (col + 1) * width)
                    if col > part:
                        work[at, to] = blocks[j]
                    elif j == 1:
                        work[to, at] = blocks[j].T

    row_ids = lax.broadcasted_iota(jnp.int32, (PANEL, 128), 0)
    lane_ids = lax.broadcasted_iota(jnp.int32, (PANEL, 128), 1)
    for r0 in range(0, n, PANEL):
        r1 = r0 + PANEL
        at, tile = r0 % 128, r0 // 128
        rows = work[r0:r1, :]
        pivots = [
            jnp.broadcast_to(rows[:, r0 + k : r0 + k + 1], (PANEL, 128)) for k in range(PANEL)
        ]
        parts = [rows[:, t : t + 128] for t in range(0, n, 128)]
        parts.append(jnp.where(lane_ids - at == row_ids, 1.0, 0.0).astype(f32))
        diagonal = jnp.ones((PANEL, 128), f32)
        for j in range(PANEL):
            pivot = pivots[j][j : j + 1, :]
            diagonal = jnp.where(row_ids == j, pivot, diagonal)
            factors = jnp.where(row_ids > j, pivots[j] * (1.0 / pivot), 0.0)
            for k in range(j + 1, PANEL):
                pivots[k] = pivots[k] - factors * pivots[k][j : j + 1, :]
            parts = [q - factors * q[j : j + 1, :] for q in parts]
        roots = lax.rsqrt(diagonal)
        parts = [q * roots for q in parts]
        in_panel = (lane_ids >= at) & (lane_ids < at + PANEL)
        joined = []
        for t in range(n // 128):
            cols = lane_ids + 128 * t
            span = slice(128 * t, 128 * t + 128)
            factor[r0:r1, span] = jnp.where(cols >= row_ids + r0, parts[t] * (1.0 / root), 0.0)
            both = jnp.where(in_panel, parts[-1], parts[t]) if t == tile else parts[t]
            joined.append(both)
            inverse[r0:r1, span] = jnp.where(cols < r1, both, 0.0)
        if r1 < n:
            h, m, l = three_parts(jnp.concatenate(joined, axis=1))
            left = jnp.concatenate([h, h, m, m, h, l], axis=0)
            right = jnp.concatenate([h, m, h, m, l, h], axis=0)
            low = r1 // 128 * 128
            update = lax.dot_general(
                left[:, low:], right, (((0,), (0,)), ((), ())), preferred_element_type=f32
            )
            cols = lax.broadcasted_iota(jnp.int32, (n - r1, n), 1)
            kept = jnp.where((cols >= r0) & (cols < r1), 0.0, work[r1:, :])
            work[r1:, :] = kept - update[r1 - low :, :]
    mine = root * inverse[pl.ds(pl.multiple_of(own * width, width), width), :]
    blocks = [mine[:, b * width : (b + 1) * width] for b in range(4)]
    ordered = []
    for k in range(4):
        source = lax.rem(own + 4 - k, 4)
        block = blocks[0]
        for b in range(1, 4):
            block = jnp.where(source == b, blocks[b], block)
        ordered.append(block)
    ordered = jnp.concatenate(ordered, axis=1)
    left = jnp.concatenate(three_parts(ordered), axis=0)
    span = basis.shape[1] // 2
    for c in range(2):
        at = slice(c * span, (c + 1) * span)
        right = jnp.concatenate(
            [finals[0][:, at], finals[1][:, at], finals[3 + c][...], finals[2][:, at]], axis=0
        )
        product = jnp.dot(left, right, preferred_element_type=f32)
        basis[:, at] = product[:width] + product[width : 2 * width] + product[2 * width :]


def solve(root, own, strips, finals):
    n = 2 * strips[0].shape[1]
    return pl.pallas_call(
        functools.partial(solve_kernel, root),
        out_shape=(
            jax.ShapeDtypeStruct(finals[0].shape, jnp.float32),
            jax.ShapeDtypeStruct((n, n), jnp.float32),
        ),
        in_specs=[smem] + [vmem] * 9,
        out_specs=(vmem,) * 2,
        scratch_shapes=[pltpu.VMEM((n, n), jnp.float32)] * 2,
        compiler_params=grant,
        name="solve",
    )(own, *strips, *finals)


def shift(value, axis, by):
    n = lax.axis_size(axis)
    return lax.ppermute(value, axis, [(i, (i + by) % n) for i in range(n)])


def swap(value, axis, mask):
    n = lax.axis_size(axis)
    return lax.ppermute(value, axis, [(i, i ^ mask) for i in range(n)])


def xor_sum(value, axis, masks):
    terms = [value] + [swap(value, axis, m) for m in masks]
    while len(terms) > 1:
        terms = [terms[i] + terms[i + 1] for i in range(0, len(terms), 2)]
    return terms[0]


def body(subspace, onsite, blocks, cols):
    row_count = lax.axis_size("row")
    row_index = lax.axis_index("row")
    col_index = lax.axis_index("col").astype(jnp.int32)
    width, local_rows = subspace.shape
    slot_count, local_blocks, size, _ = blocks.shape
    table, info = plan(cols, row_index, row_count, local_blocks)
    onsite = onsite[None, :]
    shaped = subspace.reshape(width, local_blocks, size)
    chosen = jnp.take(shaped, info[: 4 * HALO], axis=1)
    send = chosen.transpose(1, 0, 2).reshape(4, HALO, width, size)
    previous, before, x = None, subspace, subspace
    for step in range(FILTER):
        scale = filter_scale if step == 0 else 2.0 * filter_scale
        last = step == FILTER - 1
        halos = [shift(send[q], "row", -d) for q, d in enumerate(offsets(row_count))]
        partial = local_part(scale, table, blocks, x, onsite, previous)
        y, x, *send = remote_part(scale, last, info, table, halos, partial, x, blocks)
        previous, before = before, y
    final = x
    half = local_rows // 2
    one = shift(final, "col", 1)
    three = shift(final, "col", -1)
    two = [shift(one[:, :half], "col", 1), shift(three[:, half:], "col", -1)]
    strip = gram_strip(final, one, two)
    x_bit = row_count // 4
    strip = xor_sum(strip, "row", [1])
    strip = xor_sum(strip, "row", [2, 4, 6])
    strip = xor_sum(strip, "row", [x_bit, 2 * x_bit, 3 * x_bit])
    strips = [strip] + [shift(strip, "col", k) for k in (1, 2, 3)]
    root = math.sqrt(row_count * local_rows)
    return solve(root, col_index[None], strips, [final, one, three] + two)


def solution(mesh):
    in_specs = (P("col", "row"), P("row"), P(None, "row", None, None), P())
    out_specs = (P("col", "row"), P())
    return jax.shard_map(body, mesh=mesh, in_specs=in_specs, out_specs=out_specs, check_vma=False)
```

```python
import functools
import math

import jax
import jax.numpy as jnp
from jax import lax
from jax.experimental import pallas as pl
from jax.experimental.pallas import tpu as pltpu
from jax.sharding import PartitionSpec as P

HALO = 4
FILTER = 4
UNROLL = 4
LATE = 4
LOADS = 4
LANES = 128
PANEL = 16

filter_scale = 0.4


def offsets(row_count):
    return (1, -1, 2, row_count // 2)


def spread(values, s, rows):
    return jnp.broadcast_to(values[:, s : s + 1], (rows, LANES))


def ranks_of(named, local_blocks):
    hits = jnp.max(named, axis=0, keepdims=True)
    above = lax.broadcasted_iota(jnp.int32, (LANES, LANES), 0)
    here = lax.broadcasted_iota(jnp.int32, (LANES, LANES), 1)
    before = (above < here) & (above // local_blocks == here // local_blocks)
    ranks = jnp.dot(
        jnp.broadcast_to(hits, (16, LANES)).astype(jnp.bfloat16),
        jnp.where(before, 1.0, 0.0).astype(jnp.bfloat16),
        preferred_element_type=jnp.float32,
    )
    return hits, ranks[:1]


def send_kernel(row_count, at, cols, x, info, *sends):
    slot_count = cols.shape[1]
    size = sends[0].shape[2]
    local_blocks = x.shape[1] // size
    here = at[0]
    lane = lax.broadcasted_iota(jnp.int32, (local_blocks, LANES), 1)
    named = jnp.zeros((local_blocks, LANES), jnp.float32)
    for q, delta in enumerate(offsets(row_count)):
        asker = lax.rem(here + row_count - delta, row_count)
        start = pl.multiple_of(asker * local_blocks, local_blocks)
        values = cols[pl.ds(start, local_blocks), :] - (here * local_blocks - q * local_blocks)
        group = lane // local_blocks == q
        for s in range(slot_count):
            named = jnp.where(group & (spread(values, s, local_blocks) == lane), 1.0, named)
    hits, ranks = ranks_of(named, local_blocks)
    lane = lane[:1]
    for q in range(4):
        mine = (hits > 0) & (lane // local_blocks == q)
        for k in range(HALO):
            number = jnp.where(mine & (ranks == k), (lane % local_blocks).astype(jnp.float32), 0.0)
            j = jnp.sum(number).astype(jnp.int32)
            info[q * HALO + k] = j
            sends[q][k] = x[:, pl.ds(pl.multiple_of(j * size, size), size)]


def send_part(row_count, at, cols, x, size):
    send = jax.ShapeDtypeStruct((HALO, x.shape[0], size), jnp.bfloat16)
    return pl.pallas_call(
        functools.partial(send_kernel, row_count),
        out_shape=(jax.ShapeDtypeStruct((4 * HALO,), jnp.int32),) + (send,) * 4,
        in_specs=[smem] + [vmem] * 2,
        out_specs=(smem,) + (vmem,) * 4,
        compiler_params=grant,
        name="send_part",
    )(at, cols, x)


def build_table(row_count, here, values):
    rows, slot_count = values.shape
    lane = lax.broadcasted_iota(jnp.int32, (rows, LANES), 1)
    ids = jnp.zeros((rows, LANES), jnp.int32)
    for q, delta in enumerate(offsets(row_count)):
        source = lax.rem(here + row_count + delta, row_count)
        ids = jnp.where(lane // rows == q, (source - q) * rows + lane, ids)
    columns = [spread(values, s, rows) for s in range(slot_count)]
    named = jnp.zeros((rows, LANES), jnp.float32)
    near_total = jnp.zeros((rows, LANES), jnp.int32)
    nears = []
    for column in columns:
        named = jnp.where(column == ids, 1.0, named)
        within = column - here * rows
        nears.append((within >= 0) & (within < rows))
        near_total = near_total + nears[-1].astype(jnp.int32)
    _, ranks = ranks_of(named, rows)
    group = lane[:1] // rows
    places = ranks + (HALO * group + rows + 1).astype(jnp.float32)
    near_count = jnp.zeros((rows, LANES), jnp.int32)
    table = jnp.zeros((rows, LANES), jnp.int32)
    for s, (column, near) in enumerate(zip(columns, nears)):
        far = jnp.sum(jnp.where(column == ids, places, 0.0), axis=1, keepdims=True)
        place = jnp.where(near, column - here * rows, far.astype(jnp.int32))
        rank = jnp.where(near, near_count, near_total + s - near_count)
        near_count = near_count + near.astype(jnp.int32)
        table = jnp.where(lane == rank, s * 64 + place, table)
    extra = (lane < slot_count - LATE) & ((table & 63) > rows)
    count = jnp.sum(extra.astype(jnp.float32)).astype(jnp.int32)
    return jnp.where(lane == LANES // 2, count, table)


def slot_pairs(table, row, slots, held, blocks, limit):
    total = None
    for t in range(slots.start, slots.stop, 2):
        codes = [table[row, t + k] for k in range(2)]
        places = [jnp.minimum(code & 63, limit) for code in codes]
        taken = jnp.concatenate([held[p] for p in places], axis=1)
        block = jnp.concatenate([blocks[code >> 6, row] for code in codes], axis=0)
        product = jnp.dot(taken, block, preferred_element_type=jnp.float32)
        total = product if total is None else total + product
    return total


def local_rows_of(scale, table, groups, blocks, onsite, prev, y, held):
    slot_count, local_blocks, size, _ = blocks.shape

    @pl.loop(groups[0], groups[1])
    def _(group):
        for u in range(UNROLL):
            row = group * UNROLL + u
            early = range(slot_count - LATE)
            total = slot_pairs(table, row, early, held, blocks, local_blocks)
            span = pl.ds(pl.multiple_of(row * size, size), size)
            value = scale * (total + onsite[:, span] * held[row].astype(jnp.float32))
            if prev is not None:
                value = value - prev[:, span].astype(jnp.float32)
            y[:, span] = value


def hold(x, held, local_blocks):
    size = held.shape[2]
    for j in range(local_blocks):
        held[j] = x[:, j * size : (j + 1) * size]
    held[local_blocks] = jnp.zeros(held.shape[1:], held.dtype)


def local_kernel(scale, table, blocks, x, onsite, prev, y, held):
    local_blocks = blocks.shape[1]
    hold(x, held, local_blocks)
    groups = (0, local_blocks // UNROLL)
    local_rows_of(scale, table, groups, blocks, onsite, prev, y, held)


def first_kernel(scale, row_count, at, cols, far, x, onsite, y, table, blocks, held, near, sems):
    slot_count, local_blocks, _, _ = blocks.shape
    here = at[0]
    share = local_blocks // LOADS

    def rows(ref, g):
        return ref.at[:, pl.ds(g * share, share)]

    for g in range(LOADS):
        for s in range(slot_count):
            part = pl.ds(g * share, share)
            pltpu.make_async_copy(far.at[s, part], blocks.at[s, part], sems.at[g]).start()
    start = pl.multiple_of(here * local_blocks, local_blocks)
    table[...] = build_table(row_count, here, cols[pl.ds(start, local_blocks), :])
    copy = pltpu.make_async_copy(table, near, sems.at[LOADS])
    copy.start()
    hold(x, held, local_blocks)
    copy.wait()
    for g in range(LOADS):
        pltpu.make_async_copy(rows(far, g), rows(blocks, g), sems.at[g]).wait()
        groups = (g * share // UNROLL, (g + 1) * share // UNROLL)
        local_rows_of(scale, near, groups, blocks, onsite, None, y, held)


def remote_kernel(scale, keep, last, info, table, *refs):
    halos, (y_in, x_in, blocks, x), rest = refs[:4], refs[4:8], refs[8:]
    y, sends, held = (rest[0], rest[1:-1], rest[-1]) if keep else (rest[-1], rest[:-2], rest[-2])
    slot_count, local_blocks, size, _ = blocks.shape
    per = halos[0].shape[0]
    count = table[0, LANES // 2]
    hold(x_in, held, local_blocks)
    for q in range(4):
        at = local_blocks + 1 + q * per
        held[at : at + per] = halos[q][...]

    @pl.loop(0, local_blocks // UNROLL)
    def _(group):
        for u in range(UNROLL):
            row = group * UNROLL + u
            late = range(slot_count - LATE, slot_count)
            total = slot_pairs(table, row, late, held, blocks, held.shape[0] - 1)
            span = pl.ds(pl.multiple_of(row * size, size), size)
            value = y_in[:, span] + scale * total
            y[:, span] = value
            x[:, span] = value.astype(jnp.bfloat16)

    @pl.when(count > 0)
    def _():
        @pl.loop(0, local_blocks)
        def _(row):
            @pl.loop(0, slot_count - LATE)
            def _(t):
                code = table[row, t]

                @pl.when((code & 63) > local_blocks)
                def _():
                    product = jnp.dot(
                        held[code & 63], blocks[code >> 6, row], preferred_element_type=jnp.float32
                    )
                    span = pl.ds(pl.multiple_of(row * size, size), size)
                    y[:, span] = y[:, span] + scale * product

        x[...] = y[...].astype(jnp.bfloat16)

    if not last:
        for q in range(4):
            for k in range(per):
                j = info[q * per + k]
                sends[q][k] = x[:, pl.ds(pl.multiple_of(j * size, size), size)]


vmem = pl.BlockSpec(memory_space=pltpu.VMEM)
smem = pl.BlockSpec(memory_space=pltpu.SMEM)
grant = pltpu.CompilerParams(vmem_limit_bytes=16 << 20)


def local_part(scale, table, blocks, x, onsite, prev):
    _, local_blocks, size, _ = blocks.shape
    return pl.pallas_call(
        functools.partial(local_kernel, scale),
        out_shape=jax.ShapeDtypeStruct(x.shape, jnp.float32),
        in_specs=[smem] + [vmem] * 4,
        out_specs=vmem,
        scratch_shapes=[pltpu.VMEM((local_blocks + 1, x.shape[0], size), jnp.bfloat16)],
        compiler_params=grant,
        name="local_part",
    )(table, blocks, x, onsite, prev)


def first_part(scale, row_count, at, cols, blocks, x, onsite):
    _, local_blocks, size, _ = blocks.shape
    table = (local_blocks, LANES)
    return pl.pallas_call(
        functools.partial(first_kernel, scale, row_count),
        out_shape=(
            jax.ShapeDtypeStruct(x.shape, jnp.float32),
            jax.ShapeDtypeStruct(table, jnp.int32),
            jax.ShapeDtypeStruct(blocks.shape, blocks.dtype),
        ),
        in_specs=[smem, vmem, pl.BlockSpec(memory_space=pl.ANY), vmem, vmem],
        out_specs=(vmem,) * 3,
        scratch_shapes=[
            pltpu.VMEM((local_blocks + 1, x.shape[0], size), jnp.bfloat16),
            pltpu.SMEM(table, jnp.int32),
            pltpu.SemaphoreType.DMA((LOADS + 1,)),
        ],
        compiler_params=grant,
        name="first_part",
    )(at, cols, blocks, x, onsite)


def remote_part(scale, keep, last, info, table, halos, y, x, blocks):
    _, local_blocks, size, _ = blocks.shape
    width = y.shape[0]
    per = halos[0].shape[0]
    sends = () if last else (jax.ShapeDtypeStruct((per, width, size), jnp.bfloat16),) * 4
    kept = (jax.ShapeDtypeStruct(y.shape, jnp.float32),) if keep else ()
    scratch = [pltpu.VMEM((local_blocks + 1 + 4 * per, width, size), jnp.bfloat16)]
    if not keep:
        scratch.append(pltpu.VMEM(y.shape, jnp.float32))
    return pl.pallas_call(
        functools.partial(remote_kernel, scale, keep, last),
        out_shape=(jax.ShapeDtypeStruct(y.shape, jnp.bfloat16),) + kept + sends,
        in_specs=[smem] * 2 + [vmem] * 7,
        out_specs=(vmem,) * (1 + len(kept) + len(sends)),
        scratch_shapes=scratch,
        compiler_params=grant,
        name="remote_part",
    )(info, table, *halos, y, x, blocks)


def gram_kernel(own, one, three, strip):
    f32 = jnp.float32
    nt = (((1,), (1,)), ((), ()))
    width = own.shape[0]
    half = width // 2
    pair = jnp.concatenate([own[...], one[...]], axis=0)
    strip[:width, :] = lax.dot_general(own[...], pair, nt, preferred_element_type=f32)
    block = lax.dot_general(one[...], three[...], nt, preferred_element_type=f32)
    strip[width:, :] = jnp.concatenate([block[:half], block[half:]], axis=1)


def gram_strip(own, one, three):
    width = own.shape[0]
    return pl.pallas_call(
        gram_kernel,
        out_shape=jax.ShapeDtypeStruct((width + width // 2, 2 * width), jnp.float32),
        in_specs=[vmem] * 3,
        out_specs=vmem,
        compiler_params=grant,
        name="gram_strip",
    )(own, one, three)


def three_parts(value):
    high = value.astype(jnp.bfloat16)
    rest = value - high.astype(jnp.float32)
    middle = rest.astype(jnp.bfloat16)
    low = (rest - middle.astype(jnp.float32)).astype(jnp.bfloat16)
    return high, middle, low


def solve_kernel(root, own_ref, *refs):
    strips, finals, (basis, factor, work, inverse) = refs[:4], refs[4:9], refs[9:]
    own = own_ref[0]
    n = work.shape[0]
    width = n // 4
    f32 = jnp.float32
    for k in range(4):
        source = lax.rem(own + 4 - k, 4)
        for part in range(4):

            @pl.when(source == part)
            def _(part=part, strip=strips[k]):
                spans = [slice(p * width, (p + 1) * width) for p in range(4)]
                here, back, ahead = spans[part], spans[part - 1], spans[(part + 1) % 4]
                work[here, here] = strip[:width, :width]
                if part == 0:
                    work[here, back] = strip[:width, width:]
                else:
                    work[back, here] = strip[:width, width:].T
                if part in (1, 2):
                    tail = strip[width:, :]
                    work[back, ahead] = jnp.concatenate([tail[:, :width], tail[:, width:]], axis=0)

    row_ids = lax.broadcasted_iota(jnp.int32, (PANEL, 128), 0)
    lane_ids = lax.broadcasted_iota(jnp.int32, (PANEL, 128), 1)
    for r0 in range(0, n, PANEL):
        r1 = r0 + PANEL
        at, tile = r0 % 128, r0 // 128
        rows = work[r0:r1, :]
        pivots = [
            jnp.broadcast_to(rows[:, r0 + k : r0 + k + 1], (PANEL, 128)) for k in range(PANEL)
        ]
        parts = [rows[:, t : t + 128] for t in range(0, n, 128)]
        parts.append(jnp.where(lane_ids - at == row_ids, 1.0, 0.0).astype(f32))
        diagonal = jnp.ones((PANEL, 128), f32)
        for j in range(PANEL):
            pivot = pivots[j][j : j + 1, :]
            diagonal = jnp.where(row_ids == j, pivot, diagonal)
            factors = jnp.where(row_ids > j, pivots[j] * (1.0 / pivot), 0.0)
            for k in range(j + 1, PANEL):
                pivots[k] = pivots[k] - factors * pivots[k][j : j + 1, :]
            parts = [q - factors * q[j : j + 1, :] for q in parts]
        roots = lax.rsqrt(diagonal)
        parts = [q * roots for q in parts]
        in_panel = (lane_ids >= at) & (lane_ids < at + PANEL)
        joined = []
        for t in range(n // 128):
            cols = lane_ids + 128 * t
            span = slice(128 * t, 128 * t + 128)
            factor[r0:r1, span] = jnp.where(cols >= row_ids + r0, parts[t] * (1.0 / root), 0.0)
            both = jnp.where(in_panel, parts[-1], parts[t]) if t == tile else parts[t]
            joined.append(both)
            inverse[r0:r1, span] = jnp.where(cols < r1, both, 0.0)
        if r1 < n:
            h, m, l = three_parts(jnp.concatenate(joined, axis=1))
            left = jnp.concatenate([h, h, m, m, h, l], axis=0)
            right = jnp.concatenate([h, m, h, m, l, h], axis=0)
            low = r1 // 128 * 128
            update = lax.dot_general(
                left[:, low:], right, (((0,), (0,)), ((), ())), preferred_element_type=f32
            )
            cols = lax.broadcasted_iota(jnp.int32, (n - r1, n), 1)
            kept = jnp.where((cols >= r0) & (cols < r1), 0.0, work[r1:, :])
            work[r1:, :] = kept - update[r1 - low :, :]
    mine = root * inverse[pl.ds(pl.multiple_of(own * width, width), width), :]
    blocks = [mine[:, b * width : (b + 1) * width] for b in range(4)]
    ordered = []
    for k in range(4):
        source = lax.rem(own + 4 - k, 4)
        block = blocks[0]
        for b in range(1, 4):
            block = jnp.where(source == b, blocks[b], block)
        ordered.append(block)
    ordered = jnp.concatenate(ordered, axis=1)
    left = jnp.concatenate(three_parts(ordered), axis=0)
    span = basis.shape[1] // 2
    for c in range(2):
        at = slice(c * span, (c + 1) * span)
        right = jnp.concatenate(
            [finals[0][:, at], finals[1][:, at], finals[3 + c][...], finals[2][:, at]], axis=0
        )
        product = jnp.dot(left, right, preferred_element_type=f32)
        basis[:, at] = product[:width] + product[width : 2 * width] + product[2 * width :]


def solve(root, own, strips, finals):
    n = 2 * strips[0].shape[1]
    return pl.pallas_call(
        functools.partial(solve_kernel, root),
        out_shape=(
            jax.ShapeDtypeStruct(finals[0].shape, jnp.float32),
            jax.ShapeDtypeStruct((n, n), jnp.float32),
        ),
        in_specs=[smem] + [vmem] * 9,
        out_specs=(vmem,) * 2,
        scratch_shapes=[pltpu.VMEM((n, n), jnp.float32)] * 2,
        compiler_params=grant,
        name="solve",
    )(own, *strips, *finals)


def shift(value, axis, by):
    n = lax.axis_size(axis)
    return lax.ppermute(value, axis, [(i, (i + by) % n) for i in range(n)])


def swap(value, axis, mask):
    n = lax.axis_size(axis)
    return lax.ppermute(value, axis, [(i, i ^ mask) for i in range(n)])


def xor_sum(value, axis, masks):
    terms = [value] + [swap(value, axis, m) for m in masks]
    while len(terms) > 1:
        terms = [terms[i] + terms[i + 1] for i in range(0, len(terms), 2)]
    return terms[0]


def body(subspace, onsite, blocks, cols):
    row_count = lax.axis_size("row")
    row_index = lax.axis_index("row")
    col_index = lax.axis_index("col").astype(jnp.int32)
    width, local_rows = subspace.shape
    slot_count, local_blocks, size, _ = blocks.shape
    at = jnp.stack([row_index.astype(jnp.int32), col_index])
    onsite = onsite[None, :]
    info, *send = send_part(row_count, at, cols, subspace, size)
    previous, before, x = None, subspace, subspace
    for step in range(FILTER):
        scale = filter_scale if step == 0 else 2.0 * filter_scale
        last = step == FILTER - 1
        keep = step < FILTER - 2
        halos = [shift(send[q], "row", -d) for q, d in enumerate(offsets(row_count))]
        if step == 0:
            partial, table, held = first_part(scale, row_count, at, cols, blocks, x, onsite)
        else:
            partial = local_part(scale, table, held, x, onsite, previous)
        x, *send = remote_part(scale, keep, last, info, table, halos, partial, x, held)
        previous = before
        if keep:
            before, *send = send
    final = x
    half = local_rows // 2
    one = shift(final, "col", 1)
    three = shift(final, "col", -1)
    two = [shift(one[:, :half], "col", 1), shift(three[:, half:], "col", -1)]
    strip = gram_strip(final, one, three)
    x_bit = row_count // 4
    strip = xor_sum(strip, "row", [1])
    strip = xor_sum(strip, "row", [2, 4, 6])
    strip, *two = lax.optimization_barrier((strip, *two))
    strip = xor_sum(strip, "row", [x_bit, 2 * x_bit, 3 * x_bit])
    strips = [strip] + [shift(strip, "col", k) for k in (1, 2, 3)]
    root = math.sqrt(row_count * local_rows)
    return solve(root, at[1:], strips, [final, one, three] + two)


def solution(mesh):
    in_specs = (P("col", "row"), P("row"), P(None, "row", None, None), P())
    out_specs = (P("col", "row"), P())
    return jax.shard_map(body, mesh=mesh, in_specs=in_specs, out_specs=out_specs, check_vma=False)
```

```python
import functools
import math

import jax
import jax.numpy as jnp
from jax import lax
from jax.experimental import pallas as pl
from jax.experimental.pallas import tpu as pltpu
from jax.sharding import PartitionSpec as P

HALO = 4
FILTER = 4
UNROLL = 16
LATE = 4
LOADS = 8
EARLY = 1
LANES = 128
COUNT = 32
SEND = 64
PANEL = 16

filter_scale = 0.4


def offsets(row_count):
    return (1, -1, 2, row_count // 2)


def spread(values, s, rows):
    return jnp.broadcast_to(values[:, s : s + 1], (rows, LANES))


def ranks_of(named, local_blocks):
    hits = jnp.max(named, axis=0, keepdims=True)
    above = lax.broadcasted_iota(jnp.int32, (LANES, LANES), 0)
    here = lax.broadcasted_iota(jnp.int32, (LANES, LANES), 1)
    before = (above < here) & (above // local_blocks == here // local_blocks)
    ranks = jnp.dot(
        jnp.broadcast_to(hits, (16, LANES)).astype(jnp.bfloat16),
        jnp.where(before, 1.0, 0.0).astype(jnp.bfloat16),
        preferred_element_type=jnp.float32,
    )
    return hits, ranks[:1]


def load(far, blocks, sem, g):
    slot_count, local_blocks, _, _ = blocks.shape
    share = local_blocks // LOADS
    for s in range(slot_count):
        part = pl.ds(g * share, share)
        pltpu.make_async_copy(far.at[s, part], blocks.at[s, part], sem).start()


def loaded(blocks, sem, g):
    share = blocks.shape[1] // LOADS
    part = blocks.at[:, pl.ds(g * share, share)]
    pltpu.make_async_copy(part, part, sem).wait()


def send_kernel(row_count, at, far_cols, far_x, far_onsite, far, *refs):
    info, own, x, onsite, blocks, *sends, cols, turned, sems = refs
    slot_count = cols.shape[0]
    _, local_blocks, size, _ = blocks.shape
    here = at[0]
    copies = [
        pltpu.make_async_copy(far_cols, cols, sems.at[0]),
        pltpu.make_async_copy(far_x, x, sems.at[1]),
        pltpu.make_async_copy(far_onsite, onsite, sems.at[2]),
    ]
    for copy in copies:
        copy.start()
    for g in range(EARLY):
        load(far, blocks, sems.at[3 + g], g)
    copies[0].wait()
    per_tile = LANES // local_blocks

    def rows_of(device):
        start = pl.multiple_of(device // per_tile * LANES, LANES)
        tile = cols[:, pl.ds(start, LANES)]
        pad = jnp.zeros((-slot_count % 8, LANES), jnp.int32)
        turned[:, : slot_count + pad.shape[0]] = jnp.concatenate([tile, pad], axis=0).T
        start = pl.multiple_of(lax.rem(device, per_tile) * local_blocks, local_blocks)
        return turned[pl.ds(start, local_blocks), :]

    lane = lax.broadcasted_iota(jnp.int32, (local_blocks, LANES), 1)
    named = jnp.zeros((local_blocks, LANES), jnp.float32)
    for q, delta in enumerate(offsets(row_count)):
        asker = lax.rem(here + row_count - delta, row_count)
        values = rows_of(asker) - (here - q) * local_blocks
        group = lane // local_blocks == q
        for s in range(slot_count):
            named = jnp.where(group & (spread(values, s, local_blocks) == lane), 1.0, named)
    own[...] = rows_of(here)
    hits, ranks = ranks_of(named, local_blocks)
    lane = lane[:1]
    for copy in copies[1:]:
        copy.wait()
    for q in range(4):
        mine = (hits > 0) & (lane // local_blocks == q)
        for k in range(HALO):
            number = jnp.where(mine & (ranks == k), (lane % local_blocks).astype(jnp.float32), 0.0)
            j = jnp.sum(number).astype(jnp.int32)
            info[q * HALO + k] = j
            sends[q][k] = x[:, pl.ds(pl.multiple_of(j * size, size), size)]
    for g in range(EARLY):
        loaded(blocks, sems.at[3 + g], g)


def send_part(row_count, at, cols, x, onsite, blocks):
    _, local_blocks, size, _ = blocks.shape
    send = jax.ShapeDtypeStruct((HALO, x.shape[0], size), jnp.bfloat16)
    whole = [jax.ShapeDtypeStruct(v.shape, v.dtype) for v in (x, onsite, blocks)]
    hbm = pl.BlockSpec(memory_space=pltpu.HBM)
    return pl.pallas_call(
        functools.partial(send_kernel, row_count),
        out_shape=(
            jax.ShapeDtypeStruct((4 * HALO,), jnp.int32),
            jax.ShapeDtypeStruct((local_blocks, LANES), jnp.int32),
            *whole,
        )
        + (send,) * 4,
        in_specs=[smem] + [hbm] * 4,
        out_specs=(smem,) + (vmem,) * 8,
        scratch_shapes=[
            pltpu.VMEM(cols.shape, jnp.int32),
            pltpu.VMEM((LANES, LANES), jnp.int32),
            pltpu.SemaphoreType.DMA((3 + EARLY,)),
        ],
        compiler_params=grant,
        name="send_part",
    )(at, *[far_away(v) for v in (cols, x, onsite, blocks)])


def build_table(row_count, here, slot_count, values, info):
    rows = values.shape[0]
    lane = lax.broadcasted_iota(jnp.int32, (rows, LANES), 1)
    ids = jnp.zeros((rows, LANES), jnp.int32)
    for q, delta in enumerate(offsets(row_count)):
        source = lax.rem(here + row_count + delta, row_count)
        ids = jnp.where(lane // rows == q, (source - q) * rows + lane, ids)
    columns = [spread(values, s, rows) for s in range(slot_count)]
    named = jnp.zeros((rows, LANES), jnp.float32)
    near_total = jnp.zeros((rows, LANES), jnp.int32)
    nears = []
    for column in columns:
        named = jnp.where(column == ids, 1.0, named)
        within = column - here * rows
        nears.append((within >= 0) & (within < rows))
        near_total = near_total + nears[-1].astype(jnp.int32)
    _, ranks = ranks_of(named, rows)
    group = lane[:1] // rows
    places = ranks + (HALO * group + rows + 1).astype(jnp.float32)
    near_count = jnp.zeros((rows, LANES), jnp.int32)
    table = jnp.zeros((rows, LANES), jnp.int32)
    for s, (column, near) in enumerate(zip(columns, nears)):
        far = jnp.sum(jnp.where(column == ids, places, 0.0), axis=1, keepdims=True)
        place = jnp.where(near, column - here * rows, far.astype(jnp.int32))
        rank = jnp.where(near, near_count, near_total + s - near_count)
        near_count = near_count + near.astype(jnp.int32)
        table = jnp.where(lane == rank, s * 64 + place, table)
    extra = (lane < slot_count - LATE) & ((table & 63) > rows)
    count = jnp.sum(extra.astype(jnp.float32)).astype(jnp.int32)
    table = jnp.where(lane == COUNT, count, table)
    for k in range(4 * HALO):
        table = jnp.where(lane == SEND + k, info[k], table)
    return table


def slot_pairs(table, row, slots, held, blocks, limit):
    total = None
    for t in range(slots.start, slots.stop, 2):
        codes = [table[row, t + k] for k in range(2)]
        places = [jnp.minimum(code & 63, limit) for code in codes]
        taken = jnp.concatenate([held[p] for p in places], axis=1)
        block = jnp.concatenate([blocks[code >> 6, row] for code in codes], axis=0)
        product = jnp.dot(taken, block, preferred_element_type=jnp.float32)
        total = product if total is None else total + product
    return total


def local_rows_of(scale, table, groups, unroll, blocks, onsite, prev, y, held):
    slot_count, local_blocks, size, _ = blocks.shape

    @pl.loop(groups[0], groups[1])
    def _(group):
        for u in range(unroll):
            row = group * unroll + u
            early = range(slot_count - LATE)
            total = slot_pairs(table, row, early, held, blocks, local_blocks)
            span = pl.ds(pl.multiple_of(row * size, size), size)
            value = scale * (total + onsite[:, span] * held[row].astype(jnp.float32))
            if prev is not None:
                value = value - prev[:, span].astype(jnp.float32)
            y[:, span] = value


def hold(x, held, local_blocks):
    size = held.shape[2]
    for j in range(local_blocks):
        held[j] = x[:, j * size : (j + 1) * size]
    held[local_blocks] = jnp.zeros(held.shape[1:], held.dtype)


def local_kernel(scale, table, blocks, x, onsite, prev, y, held):
    local_blocks = blocks.shape[1]
    hold(x, held, local_blocks)
    groups = (0, local_blocks // UNROLL)
    local_rows_of(scale, table, groups, UNROLL, blocks, onsite, prev, y, held)


def first_kernel(scale, row_count, at, info, own, far, started, x, onsite, *refs):
    y, table, blocks, held, near, sems = refs
    slot_count, local_blocks, _, _ = blocks.shape
    share = local_blocks // LOADS
    for g in range(EARLY, LOADS):
        load(far, blocks, sems.at[g], g)
    table[...] = build_table(row_count, at[0], slot_count, own[...], info)
    copy = pltpu.make_async_copy(table, near, sems.at[LOADS])
    copy.start()
    hold(x, held, local_blocks)
    copy.wait()
    for g in range(LOADS):
        if g >= EARLY:
            loaded(blocks, sems.at[g], g)
        groups = (g, g + 1)
        local_rows_of(scale, near, groups, share, blocks, onsite, None, y, held)


def remote_kernel(scale, keep, last, table, *refs):
    halos, (y_in, x_in, blocks, x), rest = refs[:4], refs[4:8], refs[8:]
    y, sends, held = (rest[0], rest[1:-1], rest[-1]) if keep else (rest[-1], rest[:-2], rest[-2])
    slot_count, local_blocks, size, _ = blocks.shape
    per = halos[0].shape[0]
    count = table[0, COUNT]
    hold(x_in, held, local_blocks)
    for q in range(4):
        at = local_blocks + 1 + q * per
        held[at : at + per] = halos[q][...]

    @pl.loop(0, local_blocks // UNROLL)
    def _(group):
        for u in range(UNROLL):
            row = group * UNROLL + u
            late = range(slot_count - LATE, slot_count)
            total = slot_pairs(table, row, late, held, blocks, held.shape[0] - 1)
            span = pl.ds(pl.multiple_of(row * size, size), size)
            value = y_in[:, span] + scale * total
            y[:, span] = value
            x[:, span] = value.astype(jnp.bfloat16)

    @pl.when(count > 0)
    def _():
        @pl.loop(0, local_blocks)
        def _(row):
            @pl.loop(0, slot_count - LATE)
            def _(t):
                code = table[row, t]

                @pl.when((code & 63) > local_blocks)
                def _():
                    product = jnp.dot(
                        held[code & 63], blocks[code >> 6, row], preferred_element_type=jnp.float32
                    )
                    span = pl.ds(pl.multiple_of(row * size, size), size)
                    y[:, span] = y[:, span] + scale * product

        x[...] = y[...].astype(jnp.bfloat16)

    if not last:
        for q in range(4):
            for k in range(per):
                j = table[0, SEND + q * per + k]
                sends[q][k] = x[:, pl.ds(pl.multiple_of(j * size, size), size)]


vmem = pl.BlockSpec(memory_space=pltpu.VMEM)
smem = pl.BlockSpec(memory_space=pltpu.SMEM)
grant = pltpu.CompilerParams(vmem_limit_bytes=16 << 20)


def local_part(scale, table, blocks, x, onsite, prev):
    _, local_blocks, size, _ = blocks.shape
    return pl.pallas_call(
        functools.partial(local_kernel, scale),
        out_shape=jax.ShapeDtypeStruct(x.shape, jnp.float32),
        in_specs=[smem] + [vmem] * 4,
        out_specs=vmem,
        scratch_shapes=[pltpu.VMEM((local_blocks + 1, x.shape[0], size), jnp.bfloat16)],
        compiler_params=grant,
        name="local_part",
    )(table, blocks, x, onsite, prev)


def first_part(scale, row_count, at, info, own, far, started, x, onsite):
    _, local_blocks, size, _ = far.shape
    table = (local_blocks, LANES)
    hbm = pl.BlockSpec(memory_space=pltpu.HBM)
    return pl.pallas_call(
        functools.partial(first_kernel, scale, row_count),
        out_shape=(
            jax.ShapeDtypeStruct(x.shape, jnp.float32),
            jax.ShapeDtypeStruct(table, jnp.int32),
            jax.ShapeDtypeStruct(far.shape, far.dtype),
        ),
        in_specs=[smem, smem, vmem, hbm, vmem, vmem, vmem],
        out_specs=(vmem,) * 3,
        scratch_shapes=[
            pltpu.VMEM((local_blocks + 1, x.shape[0], size), jnp.bfloat16),
            pltpu.SMEM(table, jnp.int32),
            pltpu.SemaphoreType.DMA((LOADS + 1,)),
        ],
        input_output_aliases={4: 2},
        compiler_params=grant,
        name="first_part",
    )(at, info, own, far, started, x, onsite)


def remote_part(scale, keep, last, table, halos, y, x, blocks):
    _, local_blocks, size, _ = blocks.shape
    width = y.shape[0]
    per = halos[0].shape[0]
    sends = () if last else (jax.ShapeDtypeStruct((per, width, size), jnp.bfloat16),) * 4
    kept = (jax.ShapeDtypeStruct(y.shape, jnp.float32),) if keep else ()
    scratch = [pltpu.VMEM((local_blocks + 1 + 4 * per, width, size), jnp.bfloat16)]
    if not keep:
        scratch.append(pltpu.VMEM(y.shape, jnp.float32))
    return pl.pallas_call(
        functools.partial(remote_kernel, scale, keep, last),
        out_shape=(jax.ShapeDtypeStruct(y.shape, jnp.bfloat16),) + kept + sends,
        in_specs=[smem] + [vmem] * 7,
        out_specs=(vmem,) * (1 + len(kept) + len(sends)),
        scratch_shapes=scratch,
        compiler_params=grant,
        name="remote_part",
    )(table, *halos, y, x, blocks)


def gram_kernel(own, one, three, strip):
    f32 = jnp.float32
    nt = (((1,), (1,)), ((), ()))
    width = own.shape[0]
    half = width // 2
    pair = jnp.concatenate([own[...], one[...]], axis=0)
    strip[:width, :] = lax.dot_general(own[...], pair, nt, preferred_element_type=f32)
    block = lax.dot_general(one[...], three[...], nt, preferred_element_type=f32)
    strip[width:, :] = jnp.concatenate([block[:half], block[half:]], axis=1)


def gram_strip(own, one, three):
    width = own.shape[0]
    return pl.pallas_call(
        gram_kernel,
        out_shape=jax.ShapeDtypeStruct((width + width // 2, 2 * width), jnp.float32),
        in_specs=[vmem] * 3,
        out_specs=vmem,
        compiler_params=grant,
        name="gram_strip",
    )(own, one, three)


def three_parts(value):
    high = value.astype(jnp.bfloat16)
    rest = value - high.astype(jnp.float32)
    middle = rest.astype(jnp.bfloat16)
    low = (rest - middle.astype(jnp.float32)).astype(jnp.bfloat16)
    return high, middle, low


def solve_kernel(root, own_ref, *refs):
    strips, finals, (basis, factor, work, inverse) = refs[:4], refs[4:8], refs[8:]
    own = own_ref[0]
    n = work.shape[0]
    width = n // 4
    f32 = jnp.float32
    for k in range(4):
        source = lax.rem(own + 4 - k, 4)
        for part in range(4):

            @pl.when(source == part)
            def _(part=part, strip=strips[k]):
                spans = [slice(p * width, (p + 1) * width) for p in range(4)]
                here, back, ahead = spans[part], spans[part - 1], spans[(part + 1) % 4]
                work[here, here] = strip[:width, :width]
                if part == 0:
                    work[here, back] = strip[:width, width:]
                else:
                    work[back, here] = strip[:width, width:].T
                if part in (1, 2):
                    tail = strip[width:, :]
                    work[back, ahead] = jnp.concatenate([tail[:, :width], tail[:, width:]], axis=0)

    row_ids = lax.broadcasted_iota(jnp.int32, (PANEL, 128), 0)
    lane_ids = lax.broadcasted_iota(jnp.int32, (PANEL, 128), 1)
    for r0 in range(0, n, PANEL):
        r1 = r0 + PANEL
        at, tile = r0 % 128, r0 // 128
        rows = work[r0:r1, :]
        pivots = [
            jnp.broadcast_to(rows[:, r0 + k : r0 + k + 1], (PANEL, 128)) for k in range(PANEL)
        ]
        parts = [rows[:, t : t + 128] for t in range(0, n, 128)]
        parts.append(jnp.where(lane_ids - at == row_ids, 1.0, 0.0).astype(f32))
        diagonal = jnp.ones((PANEL, 128), f32)
        for j in range(PANEL):
            pivot = pivots[j][j : j + 1, :]
            diagonal = jnp.where(row_ids == j, pivot, diagonal)
            factors = jnp.where(row_ids > j, pivots[j] * (1.0 / pivot), 0.0)
            for k in range(j + 1, PANEL):
                pivots[k] = pivots[k] - factors * pivots[k][j : j + 1, :]
            parts = [q - factors * q[j : j + 1, :] for q in parts]
        roots = lax.rsqrt(diagonal)
        parts = [q * roots for q in parts]
        in_panel = (lane_ids >= at) & (lane_ids < at + PANEL)
        joined = []
        for t in range(n // 128):
            cols = lane_ids + 128 * t
            span = slice(128 * t, 128 * t + 128)
            factor[r0:r1, span] = jnp.where(cols >= row_ids + r0, parts[t] * (1.0 / root), 0.0)
            both = jnp.where(in_panel, parts[-1], parts[t]) if t == tile else parts[t]
            joined.append(both)
            inverse[r0:r1, span] = jnp.where(cols < r1, both, 0.0)
        if r1 < n:
            h, m, l = three_parts(jnp.concatenate(joined, axis=1))
            left = jnp.concatenate([h, h, m, m, h, l], axis=0)
            right = jnp.concatenate([h, m, h, m, l, h], axis=0)
            low = r1 // 128 * 128
            update = lax.dot_general(
                left[:, low:], right, (((0,), (0,)), ((), ())), preferred_element_type=f32
            )
            cols = lax.broadcasted_iota(jnp.int32, (n - r1, n), 1)
            kept = jnp.where((cols >= r0) & (cols < r1), 0.0, work[r1:, :])
            work[r1:, :] = kept - update[r1 - low :, :]
    mine = root * inverse[pl.ds(pl.multiple_of(own * width, width), width), :]
    blocks = [mine[:, b * width : (b + 1) * width] for b in range(4)]
    ordered = []
    for k in range(4):
        source = lax.rem(own + 4 - k, 4)
        block = blocks[0]
        for b in range(1, 4):
            block = jnp.where(source == b, blocks[b], block)
        ordered.append(block)
    ordered = jnp.concatenate(ordered, axis=1)
    left = jnp.concatenate(three_parts(ordered), axis=0)
    wide = 512
    for c in range(0, basis.shape[1], wide):
        right = jnp.concatenate([f[:, c : c + wide] for f in finals], axis=0)
        product = jnp.dot(left, right, preferred_element_type=f32)
        basis[:, c : c + wide] = (
            product[:width] + product[width : 2 * width] + product[2 * width :]
        )


def solve(root, own, strips, finals):
    n = 2 * strips[0].shape[1]
    return pl.pallas_call(
        functools.partial(solve_kernel, root),
        out_shape=(
            jax.ShapeDtypeStruct(finals[0].shape, jnp.float32),
            jax.ShapeDtypeStruct((n, n), jnp.float32),
        ),
        in_specs=[smem] + [vmem] * 8,
        out_specs=(vmem,) * 2,
        scratch_shapes=[pltpu.VMEM((n, n), jnp.float32)] * 2,
        compiler_params=grant,
        name="solve",
    )(own, *strips, *finals)


def shift(value, axis, by):
    n = lax.axis_size(axis)
    return lax.ppermute(value, axis, [(i, (i + by) % n) for i in range(n)])


def swap(value, axis, mask):
    n = lax.axis_size(axis)
    return lax.ppermute(value, axis, [(i, i ^ mask) for i in range(n)])


def xor_sum(value, axis, masks):
    terms = [value] + [swap(value, axis, m) for m in masks]
    while len(terms) > 1:
        terms = [terms[i] + terms[i + 1] for i in range(0, len(terms), 2)]
    return terms[0]


def far_away(value):
    return pltpu.with_memory_space_constraint(value, pltpu.HBM)


def body(subspace, onsite, blocks, cols):
    row_count = lax.axis_size("row")
    row_index = lax.axis_index("row")
    col_index = lax.axis_index("col").astype(jnp.int32)
    width, local_rows = subspace.shape
    slot_count, local_blocks, size, _ = blocks.shape
    at = jnp.stack([row_index.astype(jnp.int32), col_index])
    onsite = onsite[None, :]
    info, own, x, onsite, held, *send = send_part(row_count, at, cols.T, subspace, onsite, blocks)
    previous, before = None, x
    for step in range(FILTER):
        scale = filter_scale if step == 0 else 2.0 * filter_scale
        last = step == FILTER - 1
        keep = step < FILTER - 2
        halos = [shift(send[q], "row", -d) for q, d in enumerate(offsets(row_count))]
        if step == 0:
            partial, table, held = first_part(
                scale, row_count, at, info, own, blocks, held, x, onsite
            )
        else:
            partial = local_part(scale, table, held, x, onsite, previous)
        x, *send = remote_part(scale, keep, last, table, halos, partial, x, held)
        previous = before
        if keep:
            before, *send = send
    final = x
    one = shift(final, "col", 1)
    three = shift(final, "col", -1)
    two = shift(one, "col", 1)
    strip = gram_strip(final, one, three)
    x_bit = row_count // 4
    strip = xor_sum(strip, "row", [1])
    strip = xor_sum(strip, "row", [2, 4, 6])
    strip = xor_sum(strip, "row", [x_bit, 2 * x_bit, 3 * x_bit])
    strips = [strip] + [shift(strip, "col", k) for k in (1, 2, 3)]
    root = math.sqrt(row_count * local_rows)
    return solve(root, at[1:], strips, [final, one, two, three])


def solution(mesh):
    in_specs = (P("col", "row"), P("row"), P(None, "row", None, None), P())
    out_specs = (P("col", "row"), P())
    return jax.shard_map(body, mesh=mesh, in_specs=in_specs, out_specs=out_specs, check_vma=False)
```

```python
import functools
import math

import jax
import jax.numpy as jnp
from jax import lax
from jax.experimental import pallas as pl
from jax.experimental.pallas import tpu as pltpu
from jax.sharding import PartitionSpec as P

HALO = 4
FILTER = 4
UNROLL = 16
LATE = 4
LOADS = 8
EARLY = 1
LANES = 128
COUNT = 32
SEND = 64
PANEL = 16

filter_scale = 0.4


def beside(here, row_count):
    odd = lax.rem(here, 2)
    return [here + 1 - 2 * odd, lax.rem(here + row_count - 1 + 2 * odd, row_count)]


def sources_of(here, row_count):
    ahead = [lax.rem(here + by, row_count) for by in (2, row_count // 2)]
    return beside(here, row_count) + ahead


def askers_of(here, row_count):
    behind = [lax.rem(here + row_count - by, row_count) for by in (2, row_count // 2)]
    return beside(here, row_count) + behind


def exchange(sends, row_count):
    devices = range(row_count)
    targets = [
        [i ^ 1 for i in devices],
        [(i + 1 if i % 2 else i - 1) % row_count for i in devices],
        [(i - 2) % row_count for i in devices],
        [(i - row_count // 2) % row_count for i in devices],
    ]
    return [
        lax.ppermute(send, "row", list(zip(devices, to))) for send, to in zip(sends, targets)
    ]


def spread(values, s, rows):
    return jnp.broadcast_to(values[:, s : s + 1], (rows, LANES))


def ranks_of(named, local_blocks):
    hits = jnp.max(named, axis=0, keepdims=True)
    above = lax.broadcasted_iota(jnp.int32, (LANES, LANES), 0)
    here = lax.broadcasted_iota(jnp.int32, (LANES, LANES), 1)
    before = (above < here) & (above // local_blocks == here // local_blocks)
    ranks = jnp.dot(
        jnp.broadcast_to(hits, (16, LANES)).astype(jnp.bfloat16),
        jnp.where(before, 1.0, 0.0).astype(jnp.bfloat16),
        preferred_element_type=jnp.float32,
    )
    return hits, ranks[:1]


def load(far, blocks, sem, g):
    slot_count, local_blocks, _, _ = blocks.shape
    share = local_blocks // LOADS
    for s in range(slot_count):
        part = pl.ds(g * share, share)
        pltpu.make_async_copy(far.at[s, part], blocks.at[s, part], sem).start()


def loaded(blocks, sem, g):
    share = blocks.shape[1] // LOADS
    part = blocks.at[:, pl.ds(g * share, share)]
    pltpu.make_async_copy(part, part, sem).wait()


def send_kernel(row_count, at, far_cols, far_x, far_onsite, far, *refs):
    info, own, x, onsite, blocks, *sends, cols, turned, sems = refs
    slot_count = cols.shape[0]
    _, local_blocks, size, _ = blocks.shape
    here = at[0]
    copies = [
        pltpu.make_async_copy(far_cols, cols, sems.at[0]),
        pltpu.make_async_copy(far_x, x, sems.at[1]),
        pltpu.make_async_copy(far_onsite, onsite, sems.at[2]),
    ]
    for copy in copies:
        copy.start()
    for g in range(EARLY):
        load(far, blocks, sems.at[3 + g], g)
    copies[0].wait()
    per_tile = LANES // local_blocks

    def rows_of(device):
        start = pl.multiple_of(device // per_tile * LANES, LANES)
        tile = cols[:, pl.ds(start, LANES)]
        pad = jnp.zeros((-slot_count % 8, LANES), jnp.int32)
        turned[:, : slot_count + pad.shape[0]] = jnp.concatenate([tile, pad], axis=0).T
        start = pl.multiple_of(lax.rem(device, per_tile) * local_blocks, local_blocks)
        return turned[pl.ds(start, local_blocks), :]

    lane = lax.broadcasted_iota(jnp.int32, (local_blocks, LANES), 1)
    named = jnp.zeros((local_blocks, LANES), jnp.float32)
    for q, asker in enumerate(askers_of(here, row_count)):
        values = rows_of(asker) - (here - q) * local_blocks
        group = lane // local_blocks == q
        for s in range(slot_count):
            named = jnp.where(group & (spread(values, s, local_blocks) == lane), 1.0, named)
    own[...] = rows_of(here)
    hits, ranks = ranks_of(named, local_blocks)
    lane = lane[:1]
    for copy in copies[1:]:
        copy.wait()
    for q in range(4):
        mine = (hits > 0) & (lane // local_blocks == q)
        for k in range(HALO):
            number = jnp.where(mine & (ranks == k), (lane % local_blocks).astype(jnp.float32), 0.0)
            j = jnp.sum(number).astype(jnp.int32)
            info[q * HALO + k] = j
            sends[q][k] = x[:, pl.ds(pl.multiple_of(j * size, size), size)]
    for g in range(EARLY):
        loaded(blocks, sems.at[3 + g], g)


def send_part(row_count, at, cols, x, onsite, blocks):
    _, local_blocks, size, _ = blocks.shape
    send = jax.ShapeDtypeStruct((HALO, x.shape[0], size), jnp.bfloat16)
    whole = [jax.ShapeDtypeStruct(v.shape, v.dtype) for v in (x, onsite, blocks)]
    hbm = pl.BlockSpec(memory_space=pltpu.HBM)
    return pl.pallas_call(
        functools.partial(send_kernel, row_count),
        out_shape=(
            jax.ShapeDtypeStruct((4 * HALO,), jnp.int32),
            jax.ShapeDtypeStruct((local_blocks, LANES), jnp.int32),
            *whole,
        )
        + (send,) * 4,
        in_specs=[smem] + [hbm] * 4,
        out_specs=(smem,) + (vmem,) * 8,
        scratch_shapes=[
            pltpu.VMEM(cols.shape, jnp.int32),
            pltpu.VMEM((LANES, LANES), jnp.int32),
            pltpu.SemaphoreType.DMA((3 + EARLY,)),
        ],
        compiler_params=grant,
        name="send_part",
    )(at, *[far_away(v) for v in (cols, x, onsite, blocks)])


def build_table(row_count, here, slot_count, values, info):
    rows = values.shape[0]
    lane = lax.broadcasted_iota(jnp.int32, (rows, LANES), 1)
    ids = jnp.zeros((rows, LANES), jnp.int32)
    for q, source in enumerate(sources_of(here, row_count)):
        ids = jnp.where(lane // rows == q, (source - q) * rows + lane, ids)
    columns = [spread(values, s, rows) for s in range(slot_count)]
    named = jnp.zeros((rows, LANES), jnp.float32)
    near_total = jnp.zeros((rows, LANES), jnp.int32)
    nears = []
    for column in columns:
        named = jnp.where(column == ids, 1.0, named)
        within = column - here * rows
        nears.append((within >= 0) & (within < rows))
        near_total = near_total + nears[-1].astype(jnp.int32)
    _, ranks = ranks_of(named, rows)
    group = lane[:1] // rows
    places = ranks + (HALO * group + rows + 1).astype(jnp.float32)
    near_count = jnp.zeros((rows, LANES), jnp.int32)
    table = jnp.zeros((rows, LANES), jnp.int32)
    for s, (column, near) in enumerate(zip(columns, nears)):
        far = jnp.sum(jnp.where(column == ids, places, 0.0), axis=1, keepdims=True)
        place = jnp.where(near, column - here * rows, far.astype(jnp.int32))
        rank = jnp.where(near, near_count, near_total + s - near_count)
        near_count = near_count + near.astype(jnp.int32)
        table = jnp.where(lane == rank, s * 64 + place, table)
    extra = (lane < slot_count - LATE) & ((table & 63) > rows)
    count = jnp.sum(extra.astype(jnp.float32)).astype(jnp.int32)
    table = jnp.where(lane == COUNT, count, table)
    for k in range(4 * HALO):
        table = jnp.where(lane == SEND + k, info[k], table)
    return table


def slot_pairs(table, row, slots, held, blocks, limit):
    total = None
    for t in range(slots.start, slots.stop, 2):
        codes = [table[row, t + k] for k in range(2)]
        places = [jnp.minimum(code & 63, limit) for code in codes]
        taken = jnp.concatenate([held[p] for p in places], axis=1)
        block = jnp.concatenate([blocks[code >> 6, row] for code in codes], axis=0)
        product = jnp.dot(taken, block, preferred_element_type=jnp.float32)
        total = product if total is None else total + product
    return total


def local_rows_of(scale, table, groups, unroll, blocks, onsite, prev, y, held):
    slot_count, local_blocks, size, _ = blocks.shape

    @pl.loop(groups[0], groups[1])
    def _(group):
        for u in range(unroll):
            row = group * unroll + u
            early = range(slot_count - LATE)
            total = slot_pairs(table, row, early, held, blocks, local_blocks)
            span = pl.ds(pl.multiple_of(row * size, size), size)
            value = scale * (total + onsite[:, span] * held[row].astype(jnp.float32))
            if prev is not None:
                value = value - prev[:, span].astype(jnp.float32)
            y[:, span] = value


def hold(x, held, local_blocks):
    size = held.shape[2]
    for j in range(local_blocks):
        held[j] = x[:, j * size : (j + 1) * size]
    held[local_blocks] = jnp.zeros(held.shape[1:], held.dtype)


def local_kernel(scale, table, blocks, x, onsite, prev, y, held):
    local_blocks = blocks.shape[1]
    hold(x, held, local_blocks)
    groups = (0, local_blocks // UNROLL)
    local_rows_of(scale, table, groups, UNROLL, blocks, onsite, prev, y, held)


def first_kernel(scale, row_count, at, info, own, far, started, x, onsite, *refs):
    y, table, blocks, held, near, sems = refs
    slot_count, local_blocks, _, _ = blocks.shape
    share = local_blocks // LOADS
    for g in range(EARLY, LOADS):
        load(far, blocks, sems.at[g], g)
    table[...] = build_table(row_count, at[0], slot_count, own[...], info)
    copy = pltpu.make_async_copy(table, near, sems.at[LOADS])
    copy.start()
    hold(x, held, local_blocks)
    copy.wait()
    for g in range(LOADS):
        if g >= EARLY:
            loaded(blocks, sems.at[g], g)
        groups = (g, g + 1)
        local_rows_of(scale, near, groups, share, blocks, onsite, None, y, held)


def remote_kernel(scale, keep, last, table, *refs):
    halos, (y_in, x_in, blocks, x), rest = refs[:4], refs[4:8], refs[8:]
    y, sends, held = (rest[0], rest[1:-1], rest[-1]) if keep else (rest[-1], rest[:-2], rest[-2])
    slot_count, local_blocks, size, _ = blocks.shape
    per = halos[0].shape[0]
    count = table[0, COUNT]
    hold(x_in, held, local_blocks)
    for q in range(4):
        at = local_blocks + 1 + q * per
        held[at : at + per] = halos[q][...]

    @pl.loop(0, local_blocks // UNROLL)
    def _(group):
        for u in range(UNROLL):
            row = group * UNROLL + u
            late = range(slot_count - LATE, slot_count)
            total = slot_pairs(table, row, late, held, blocks, held.shape[0] - 1)
            span = pl.ds(pl.multiple_of(row * size, size), size)
            value = y_in[:, span] + scale * total
            y[:, span] = value
            x[:, span] = value.astype(jnp.bfloat16)

    @pl.when(count > 0)
    def _():
        @pl.loop(0, local_blocks)
        def _(row):
            @pl.loop(0, slot_count - LATE)
            def _(t):
                code = table[row, t]

                @pl.when((code & 63) > local_blocks)
                def _():
                    product = jnp.dot(
                        held[code & 63], blocks[code >> 6, row], preferred_element_type=jnp.float32
                    )
                    span = pl.ds(pl.multiple_of(row * size, size), size)
                    y[:, span] = y[:, span] + scale * product

        x[...] = y[...].astype(jnp.bfloat16)

    if not last:
        for q in range(4):
            for k in range(per):
                j = table[0, SEND + q * per + k]
                sends[q][k] = x[:, pl.ds(pl.multiple_of(j * size, size), size)]


vmem = pl.BlockSpec(memory_space=pltpu.VMEM)
smem = pl.BlockSpec(memory_space=pltpu.SMEM)
grant = pltpu.CompilerParams(vmem_limit_bytes=16 << 20)


def local_part(scale, table, blocks, x, onsite, prev):
    _, local_blocks, size, _ = blocks.shape
    return pl.pallas_call(
        functools.partial(local_kernel, scale),
        out_shape=jax.ShapeDtypeStruct(x.shape, jnp.float32),
        in_specs=[smem] + [vmem] * 4,
        out_specs=vmem,
        scratch_shapes=[pltpu.VMEM((local_blocks + 1, x.shape[0], size), jnp.bfloat16)],
        compiler_params=grant,
        name="local_part",
    )(table, blocks, x, onsite, prev)


def first_part(scale, row_count, at, info, own, far, started, x, onsite):
    _, local_blocks, size, _ = far.shape
    table = (local_blocks, LANES)
    hbm = pl.BlockSpec(memory_space=pltpu.HBM)
    return pl.pallas_call(
        functools.partial(first_kernel, scale, row_count),
        out_shape=(
            jax.ShapeDtypeStruct(x.shape, jnp.float32),
            jax.ShapeDtypeStruct(table, jnp.int32),
            jax.ShapeDtypeStruct(far.shape, far.dtype),
        ),
        in_specs=[smem, smem, vmem, hbm, vmem, vmem, vmem],
        out_specs=(vmem,) * 3,
        scratch_shapes=[
            pltpu.VMEM((local_blocks + 1, x.shape[0], size), jnp.bfloat16),
            pltpu.SMEM(table, jnp.int32),
            pltpu.SemaphoreType.DMA((LOADS + 1,)),
        ],
        input_output_aliases={4: 2},
        compiler_params=grant,
        name="first_part",
    )(at, info, own, far, started, x, onsite)


def remote_part(scale, keep, last, table, halos, y, x, blocks):
    _, local_blocks, size, _ = blocks.shape
    width = y.shape[0]
    per = halos[0].shape[0]
    sends = () if last else (jax.ShapeDtypeStruct((per, width, size), jnp.bfloat16),) * 4
    kept = (jax.ShapeDtypeStruct(y.shape, jnp.float32),) if keep else ()
    scratch = [pltpu.VMEM((local_blocks + 1 + 4 * per, width, size), jnp.bfloat16)]
    if not keep:
        scratch.append(pltpu.VMEM(y.shape, jnp.float32))
    return pl.pallas_call(
        functools.partial(remote_kernel, scale, keep, last),
        out_shape=(jax.ShapeDtypeStruct(y.shape, jnp.bfloat16),) + kept + sends,
        in_specs=[smem] + [vmem] * 7,
        out_specs=(vmem,) * (1 + len(kept) + len(sends)),
        scratch_shapes=scratch,
        compiler_params=grant,
        name="remote_part",
    )(table, *halos, y, x, blocks)


def gram_kernel(own, one, three, strip):
    f32 = jnp.float32
    nt = (((1,), (1,)), ((), ()))
    width = own.shape[0]
    half = width // 2
    pair = jnp.concatenate([own[...], one[...]], axis=0)
    strip[:width, :] = lax.dot_general(own[...], pair, nt, preferred_element_type=f32)
    block = lax.dot_general(one[...], three[...], nt, preferred_element_type=f32)
    strip[width:, :] = jnp.concatenate([block[:half], block[half:]], axis=1)


def gram_strip(own, one, three):
    width = own.shape[0]
    return pl.pallas_call(
        gram_kernel,
        out_shape=jax.ShapeDtypeStruct((width + width // 2, 2 * width), jnp.float32),
        in_specs=[vmem] * 3,
        out_specs=vmem,
        compiler_params=grant,
        name="gram_strip",
    )(own, one, three)


def three_parts(value):
    high = value.astype(jnp.bfloat16)
    rest = value - high.astype(jnp.float32)
    middle = rest.astype(jnp.bfloat16)
    low = (rest - middle.astype(jnp.float32)).astype(jnp.bfloat16)
    return high, middle, low


def solve_kernel(root, own_ref, *refs):
    strips, finals, (basis, factor, work, inverse) = refs[:4], refs[4:8], refs[8:]
    own = own_ref[0]
    n = work.shape[0]
    width = n // 4
    f32 = jnp.float32
    for k in range(4):
        source = lax.rem(own + 4 - k, 4)
        for part in range(4):

            @pl.when(source == part)
            def _(part=part, strip=strips[k]):
                spans = [slice(p * width, (p + 1) * width) for p in range(4)]
                here, back, ahead = spans[part], spans[part - 1], spans[(part + 1) % 4]
                work[here, here] = strip[:width, :width]
                if part == 0:
                    work[here, back] = strip[:width, width:]
                else:
                    work[back, here] = strip[:width, width:].T
                if part in (1, 2):
                    tail = strip[width:, :]
                    work[back, ahead] = jnp.concatenate([tail[:, :width], tail[:, width:]], axis=0)

    row_ids = lax.broadcasted_iota(jnp.int32, (PANEL, 128), 0)
    lane_ids = lax.broadcasted_iota(jnp.int32, (PANEL, 128), 1)
    for r0 in range(0, n, PANEL):
        r1 = r0 + PANEL
        at, tile = r0 % 128, r0 // 128
        rows = work[r0:r1, :]
        pivots = [
            jnp.broadcast_to(rows[:, r0 + k : r0 + k + 1], (PANEL, 128)) for k in range(PANEL)
        ]
        parts = [rows[:, t : t + 128] for t in range(0, n, 128)]
        parts.append(jnp.where(lane_ids - at == row_ids, 1.0, 0.0).astype(f32))
        diagonal = jnp.ones((PANEL, 128), f32)
        for j in range(PANEL):
            pivot = pivots[j][j : j + 1, :]
            diagonal = jnp.where(row_ids == j, pivot, diagonal)
            factors = jnp.where(row_ids > j, pivots[j] * (1.0 / pivot), 0.0)
            for k in range(j + 1, PANEL):
                pivots[k] = pivots[k] - factors * pivots[k][j : j + 1, :]
            parts = [q - factors * q[j : j + 1, :] for q in parts]
        roots = lax.rsqrt(diagonal)
        parts = [q * roots for q in parts]
        in_panel = (lane_ids >= at) & (lane_ids < at + PANEL)
        joined = []
        for t in range(n // 128):
            cols = lane_ids + 128 * t
            span = slice(128 * t, 128 * t + 128)
            factor[r0:r1, span] = jnp.where(cols >= row_ids + r0, parts[t] * (1.0 / root), 0.0)
            both = jnp.where(in_panel, parts[-1], parts[t]) if t == tile else parts[t]
            joined.append(both)
            inverse[r0:r1, span] = jnp.where(cols < r1, both, 0.0)
        if r1 < n:
            h, m, l = three_parts(jnp.concatenate(joined, axis=1))
            left = jnp.concatenate([h, h, m, m, h, l], axis=0)
            right = jnp.concatenate([h, m, h, m, l, h], axis=0)
            low = r1 // 128 * 128
            update = lax.dot_general(
                left[:, low:], right, (((0,), (0,)), ((), ())), preferred_element_type=f32
            )
            cols = lax.broadcasted_iota(jnp.int32, (n - r1, n), 1)
            kept = jnp.where((cols >= r0) & (cols < r1), 0.0, work[r1:, :])
            work[r1:, :] = kept - update[r1 - low :, :]
    mine = root * inverse[pl.ds(pl.multiple_of(own * width, width), width), :]
    blocks = [mine[:, b * width : (b + 1) * width] for b in range(4)]
    ordered = []
    for k in range(4):
        source = lax.rem(own + 4 - k, 4)
        block = blocks[0]
        for b in range(1, 4):
            block = jnp.where(source == b, blocks[b], block)
        ordered.append(block)
    ordered = jnp.concatenate(ordered, axis=1)
    left = jnp.concatenate(three_parts(ordered), axis=0)
    wide = 512
    for c in range(0, basis.shape[1], wide):
        right = jnp.concatenate([f[:, c : c + wide] for f in finals], axis=0)
        product = jnp.dot(left, right, preferred_element_type=f32)
        basis[:, c : c + wide] = (
            product[:width] + product[width : 2 * width] + product[2 * width :]
        )


def solve(root, own, strips, finals):
    n = 2 * strips[0].shape[1]
    return pl.pallas_call(
        functools.partial(solve_kernel, root),
        out_shape=(
            jax.ShapeDtypeStruct(finals[0].shape, jnp.float32),
            jax.ShapeDtypeStruct((n, n), jnp.float32),
        ),
        in_specs=[smem] + [vmem] * 8,
        out_specs=(vmem,) * 2,
        scratch_shapes=[pltpu.VMEM((n, n), jnp.float32)] * 2,
        compiler_params=grant,
        name="solve",
    )(own, *strips, *finals)


def shift(value, axis, by):
    n = lax.axis_size(axis)
    return lax.ppermute(value, axis, [(i, (i + by) % n) for i in range(n)])


def swap(value, axis, mask):
    n = lax.axis_size(axis)
    return lax.ppermute(value, axis, [(i, i ^ mask) for i in range(n)])


def xor_sum(value, axis, masks):
    terms = [value] + [swap(value, axis, m) for m in masks]
    while len(terms) > 1:
        terms = [terms[i] + terms[i + 1] for i in range(0, len(terms), 2)]
    return terms[0]


def far_away(value):
    return pltpu.with_memory_space_constraint(value, pltpu.HBM)


def body(subspace, onsite, blocks, cols):
    row_count = lax.axis_size("row")
    row_index = lax.axis_index("row")
    col_index = lax.axis_index("col").astype(jnp.int32)
    width, local_rows = subspace.shape
    slot_count, local_blocks, size, _ = blocks.shape
    at = jnp.stack([row_index.astype(jnp.int32), col_index])
    onsite = onsite[None, :]
    info, own, x, onsite, held, *send = send_part(row_count, at, cols.T, subspace, onsite, blocks)
    previous, before = None, x
    for step in range(FILTER):
        scale = filter_scale if step == 0 else 2.0 * filter_scale
        last = step == FILTER - 1
        keep = step < FILTER - 2
        halos = exchange(send, row_count)
        if step == 0:
            partial, table, held = first_part(
                scale, row_count, at, info, own, blocks, held, x, onsite
            )
        else:
            partial = local_part(scale, table, held, x, onsite, previous)
        x, *send = remote_part(scale, keep, last, table, halos, partial, x, held)
        previous = before
        if keep:
            before, *send = send
    final = x
    one = shift(final, "col", 1)
    three = shift(final, "col", -1)
    two = shift(one, "col", 1)
    strip = gram_strip(final, one, three)
    x_bit = row_count // 4
    strip = xor_sum(strip, "row", [1])
    strip = xor_sum(strip, "row", [2, 4, 6])
    strip = xor_sum(strip, "row", [x_bit, 2 * x_bit, 3 * x_bit])
    strips = [strip] + [shift(strip, "col", k) for k in (1, 2, 3)]
    root = math.sqrt(row_count * local_rows)
    return solve(root, at[1:], strips, [final, one, two, three])


def solution(mesh):
    in_specs = (P("col", "row"), P("row"), P(None, "row", None, None), P())
    out_specs = (P("col", "row"), P())
    return jax.shard_map(body, mesh=mesh, in_specs=in_specs, out_specs=out_specs, check_vma=False)
```

```python
import functools
import math

import jax
import jax.numpy as jnp
from jax import lax
from jax.experimental import pallas as pl
from jax.experimental.pallas import tpu as pltpu
from jax.sharding import PartitionSpec as P

HALO = 4
FILTER = 4
UNROLL = 16
LATE = 4
LOADS = 8
EARLY = 1
LANES = 128
COUNT = 32
SEND = 64
PANEL = 16
PIECES = 4

filter_scale = 0.4


def beside(here, row_count):
    odd = lax.rem(here, 2)
    return [here + 1 - 2 * odd, lax.rem(here + row_count - 1 + 2 * odd, row_count)]


def sources_of(here, row_count):
    ahead = [lax.rem(here + by, row_count) for by in (2, row_count // 2)]
    return beside(here, row_count) + ahead


def askers_of(here, row_count):
    behind = [lax.rem(here + row_count - by, row_count) for by in (2, row_count // 2)]
    return beside(here, row_count) + behind


def exchange(sends, row_count):
    devices = range(row_count)
    targets = [
        [i ^ 1 for i in devices],
        [(i + 1 if i % 2 else i - 1) % row_count for i in devices],
        [(i - 2) % row_count for i in devices],
        [(i - row_count // 2) % row_count for i in devices],
    ]
    return [
        lax.ppermute(send, "row", list(zip(devices, to))) for send, to in zip(sends, targets)
    ]


def spread(values, s, rows):
    return jnp.broadcast_to(values[:, s : s + 1], (rows, LANES))


def ranks_of(named, local_blocks):
    hits = jnp.max(named, axis=0, keepdims=True)
    above = lax.broadcasted_iota(jnp.int32, (LANES, LANES), 0)
    here = lax.broadcasted_iota(jnp.int32, (LANES, LANES), 1)
    before = (above < here) & (above // local_blocks == here // local_blocks)
    ranks = jnp.dot(
        jnp.broadcast_to(hits, (16, LANES)).astype(jnp.bfloat16),
        jnp.where(before, 1.0, 0.0).astype(jnp.bfloat16),
        preferred_element_type=jnp.float32,
    )
    return hits, ranks[:1]


def load(far, blocks, sem, g):
    slot_count, local_blocks, _, _ = blocks.shape
    share = local_blocks // LOADS
    for s in range(slot_count):
        part = pl.ds(g * share, share)
        pltpu.make_async_copy(far.at[s, part], blocks.at[s, part], sem).start()


def loaded(blocks, sem, g):
    share = blocks.shape[1] // LOADS
    part = blocks.at[:, pl.ds(g * share, share)]
    pltpu.make_async_copy(part, part, sem).wait()


def send_kernel(row_count, at, far_cols, far_x, far_onsite, far, *refs):
    info, own, x, onsite, blocks, *sends, cols, turned, sems = refs
    slot_count = cols.shape[0]
    _, local_blocks, size, _ = blocks.shape
    here = at[0]
    copies = [
        pltpu.make_async_copy(far_cols, cols, sems.at[0]),
        pltpu.make_async_copy(far_x, x, sems.at[1]),
        pltpu.make_async_copy(far_onsite, onsite, sems.at[2]),
    ]
    for copy in copies:
        copy.start()
    for g in range(EARLY):
        load(far, blocks, sems.at[3 + g], g)
    copies[0].wait()
    per_tile = LANES // local_blocks

    def rows_of(device):
        start = pl.multiple_of(device // per_tile * LANES, LANES)
        tile = cols[:, pl.ds(start, LANES)]
        pad = jnp.zeros((-slot_count % 8, LANES), jnp.int32)
        turned[:, : slot_count + pad.shape[0]] = jnp.concatenate([tile, pad], axis=0).T
        start = pl.multiple_of(lax.rem(device, per_tile) * local_blocks, local_blocks)
        return turned[pl.ds(start, local_blocks), :]

    lane = lax.broadcasted_iota(jnp.int32, (local_blocks, LANES), 1)
    named = jnp.zeros((local_blocks, LANES), jnp.float32)
    for q, asker in enumerate(askers_of(here, row_count)):
        values = rows_of(asker) - (here - q) * local_blocks
        group = lane // local_blocks == q
        for s in range(slot_count):
            named = jnp.where(group & (spread(values, s, local_blocks) == lane), 1.0, named)
    own[...] = rows_of(here)
    hits, ranks = ranks_of(named, local_blocks)
    entry = lax.broadcasted_iota(jnp.int32, (4 * HALO, LANES), 0)
    lane = lax.broadcasted_iota(jnp.int32, (4 * HALO, LANES), 1)
    chosen = (hits > 0) & (lane // local_blocks == entry // HALO)
    chosen = chosen & (ranks.astype(jnp.int32) == entry % HALO)
    numbers = jnp.where(chosen, (lane % local_blocks).astype(jnp.float32), 0.0)
    numbers = jnp.sum(numbers, axis=1, keepdims=True).astype(jnp.int32)
    for copy in copies[1:]:
        copy.wait()
    for q in range(4):
        for k in range(HALO):
            j = numbers[q * HALO + k, 0]
            info[q * HALO + k] = j
            sends[q][k] = x[:, pl.ds(pl.multiple_of(j * size, size), size)]
    for g in range(EARLY):
        loaded(blocks, sems.at[3 + g], g)


def send_part(row_count, at, cols, x, onsite, blocks):
    _, local_blocks, size, _ = blocks.shape
    send = jax.ShapeDtypeStruct((HALO, x.shape[0], size), jnp.bfloat16)
    whole = [jax.ShapeDtypeStruct(v.shape, v.dtype) for v in (x, onsite, blocks)]
    hbm = pl.BlockSpec(memory_space=pltpu.HBM)
    return pl.pallas_call(
        functools.partial(send_kernel, row_count),
        out_shape=(
            jax.ShapeDtypeStruct((4 * HALO,), jnp.int32),
            jax.ShapeDtypeStruct((local_blocks, LANES), jnp.int32),
            *whole,
        )
        + (send,) * 4,
        in_specs=[smem] + [hbm] * 4,
        out_specs=(smem,) + (vmem,) * 8,
        scratch_shapes=[
            pltpu.VMEM(cols.shape, jnp.int32),
            pltpu.VMEM((LANES, LANES), jnp.int32),
            pltpu.SemaphoreType.DMA((3 + EARLY,)),
        ],
        compiler_params=grant,
        name="send_part",
    )(at, *[far_away(v) for v in (cols, x, onsite, blocks)])


def build_table(row_count, here, slot_count, values, info):
    rows = values.shape[0]
    lane = lax.broadcasted_iota(jnp.int32, (rows, LANES), 1)
    ids = jnp.zeros((rows, LANES), jnp.int32)
    for q, source in enumerate(sources_of(here, row_count)):
        ids = jnp.where(lane // rows == q, (source - q) * rows + lane, ids)
    columns = [spread(values, s, rows) for s in range(slot_count)]
    named = jnp.zeros((rows, LANES), jnp.float32)
    near_total = jnp.zeros((rows, LANES), jnp.int32)
    nears = []
    for column in columns:
        named = jnp.where(column == ids, 1.0, named)
        within = column - here * rows
        nears.append((within >= 0) & (within < rows))
        near_total = near_total + nears[-1].astype(jnp.int32)
    _, ranks = ranks_of(named, rows)
    group = lane[:1] // rows
    places = ranks + (HALO * group + rows + 1).astype(jnp.float32)
    near_count = jnp.zeros((rows, LANES), jnp.int32)
    table = jnp.zeros((rows, LANES), jnp.int32)
    for s, (column, near) in enumerate(zip(columns, nears)):
        far = jnp.sum(jnp.where(column == ids, places, 0.0), axis=1, keepdims=True)
        place = jnp.where(near, column - here * rows, far.astype(jnp.int32))
        rank = jnp.where(near, near_count, near_total + s - near_count)
        near_count = near_count + near.astype(jnp.int32)
        table = jnp.where(lane == rank, s * 64 + place, table)
    extra = (lane < slot_count - LATE) & ((table & 63) > rows)
    count = jnp.sum(extra.astype(jnp.float32)).astype(jnp.int32)
    table = jnp.where(lane == COUNT, count, table)
    for k in range(4 * HALO):
        table = jnp.where(lane == SEND + k, info[k], table)
    return table


def slot_pairs(table, row, slots, held, blocks, limit):
    total = None
    for t in range(slots.start, slots.stop, 2):
        codes = [table[row, t + k] for k in range(2)]
        places = [jnp.minimum(code & 63, limit) for code in codes]
        taken = jnp.concatenate([held[p] for p in places], axis=1)
        block = jnp.concatenate([blocks[code >> 6, row] for code in codes], axis=0)
        product = jnp.dot(taken, block, preferred_element_type=jnp.float32)
        total = product if total is None else total + product
    return total


def local_rows_of(scale, table, groups, unroll, blocks, onsite, prev, y, held):
    slot_count, local_blocks, size, _ = blocks.shape

    @pl.loop(groups[0], groups[1])
    def _(group):
        for u in range(unroll):
            row = group * unroll + u
            early = range(slot_count - LATE)
            total = slot_pairs(table, row, early, held, blocks, local_blocks)
            span = pl.ds(pl.multiple_of(row * size, size), size)
            value = scale * (total + onsite[:, span] * held[row].astype(jnp.float32))
            if prev is not None:
                value = value - prev[:, span].astype(jnp.float32)
            y[:, span] = value


def hold(x, held, local_blocks):
    size = held.shape[2]
    for j in range(local_blocks):
        held[j] = x[:, j * size : (j + 1) * size]
    held[local_blocks] = jnp.zeros(held.shape[1:], held.dtype)


def local_kernel(scale, table, blocks, x, onsite, prev, y, held):
    local_blocks = blocks.shape[1]
    hold(x, held, local_blocks)
    groups = (0, local_blocks // UNROLL)
    local_rows_of(scale, table, groups, UNROLL, blocks, onsite, prev, y, held)


def first_kernel(scale, row_count, at, info, own, far, started, x, onsite, *refs):
    y, table, blocks, held, near, sems = refs
    slot_count, local_blocks, _, _ = blocks.shape
    share = local_blocks // LOADS
    for g in range(EARLY, LOADS):
        load(far, blocks, sems.at[g], g)
    table[...] = build_table(row_count, at[0], slot_count, own[...], info)
    copy = pltpu.make_async_copy(table, near, sems.at[LOADS])
    copy.start()
    hold(x, held, local_blocks)
    copy.wait()
    for g in range(LOADS):
        if g >= EARLY:
            loaded(blocks, sems.at[g], g)
        groups = (g, g + 1)
        local_rows_of(scale, near, groups, share, blocks, onsite, None, y, held)


def remote_kernel(scale, keep, last, table, *refs):
    halos, (y_in, x_in, blocks, x), rest = refs[:4], refs[4:8], refs[8:]
    y, sends, held = (rest[0], rest[1:-1], rest[-1]) if keep else (rest[-1], rest[:-2], rest[-2])
    slot_count, local_blocks, size, _ = blocks.shape
    per = halos[0].shape[0]
    count = table[0, COUNT]
    hold(x_in, held, local_blocks)
    for q in range(4):
        at = local_blocks + 1 + q * per
        held[at : at + per] = halos[q][...]

    @pl.loop(0, local_blocks // UNROLL)
    def _(group):
        for u in range(UNROLL):
            row = group * UNROLL + u
            late = range(slot_count - LATE, slot_count)
            total = slot_pairs(table, row, late, held, blocks, held.shape[0] - 1)
            span = pl.ds(pl.multiple_of(row * size, size), size)
            value = y_in[:, span] + scale * total
            y[:, span] = value
            x[:, span] = value.astype(jnp.bfloat16)

    @pl.when(count > 0)
    def _():
        @pl.loop(0, local_blocks)
        def _(row):
            @pl.loop(0, slot_count - LATE)
            def _(t):
                code = table[row, t]

                @pl.when((code & 63) > local_blocks)
                def _():
                    product = jnp.dot(
                        held[code & 63], blocks[code >> 6, row], preferred_element_type=jnp.float32
                    )
                    span = pl.ds(pl.multiple_of(row * size, size), size)
                    y[:, span] = y[:, span] + scale * product

        x[...] = y[...].astype(jnp.bfloat16)

    if not last:
        for q in range(4):
            for k in range(per):
                j = table[0, SEND + q * per + k]
                sends[q][k] = x[:, pl.ds(pl.multiple_of(j * size, size), size)]


vmem = pl.BlockSpec(memory_space=pltpu.VMEM)
smem = pl.BlockSpec(memory_space=pltpu.SMEM)
grant = pltpu.CompilerParams(vmem_limit_bytes=16 << 20)


def local_part(scale, table, blocks, x, onsite, prev):
    _, local_blocks, size, _ = blocks.shape
    return pl.pallas_call(
        functools.partial(local_kernel, scale),
        out_shape=jax.ShapeDtypeStruct(x.shape, jnp.float32),
        in_specs=[smem] + [vmem] * 4,
        out_specs=vmem,
        scratch_shapes=[pltpu.VMEM((local_blocks + 1, x.shape[0], size), jnp.bfloat16)],
        compiler_params=grant,
        name="local_part",
    )(table, blocks, x, onsite, prev)


def first_part(scale, row_count, at, info, own, far, started, x, onsite):
    _, local_blocks, size, _ = far.shape
    table = (local_blocks, LANES)
    hbm = pl.BlockSpec(memory_space=pltpu.HBM)
    return pl.pallas_call(
        functools.partial(first_kernel, scale, row_count),
        out_shape=(
            jax.ShapeDtypeStruct(x.shape, jnp.float32),
            jax.ShapeDtypeStruct(table, jnp.int32),
            jax.ShapeDtypeStruct(far.shape, far.dtype),
        ),
        in_specs=[smem, smem, vmem, hbm, vmem, vmem, vmem],
        out_specs=(vmem,) * 3,
        scratch_shapes=[
            pltpu.VMEM((local_blocks + 1, x.shape[0], size), jnp.bfloat16),
            pltpu.SMEM(table, jnp.int32),
            pltpu.SemaphoreType.DMA((LOADS + 1,)),
        ],
        input_output_aliases={4: 2},
        compiler_params=grant,
        name="first_part",
    )(at, info, own, far, started, x, onsite)


def remote_part(scale, keep, last, table, halos, y, x, blocks):
    _, local_blocks, size, _ = blocks.shape
    width = y.shape[0]
    per = halos[0].shape[0]
    sends = () if last else (jax.ShapeDtypeStruct((per, width, size), jnp.bfloat16),) * 4
    kept = (jax.ShapeDtypeStruct(y.shape, jnp.float32),) if keep else ()
    scratch = [pltpu.VMEM((local_blocks + 1 + 4 * per, width, size), jnp.bfloat16)]
    if not keep:
        scratch.append(pltpu.VMEM(y.shape, jnp.float32))
    return pl.pallas_call(
        functools.partial(remote_kernel, scale, keep, last),
        out_shape=(jax.ShapeDtypeStruct(y.shape, jnp.bfloat16),) + kept + sends,
        in_specs=[smem] + [vmem] * 7,
        out_specs=(vmem,) * (1 + len(kept) + len(sends)),
        scratch_shapes=scratch,
        compiler_params=grant,
        name="remote_part",
    )(table, *halos, y, x, blocks)


def gram_kernel(own, one, three, strip):
    f32 = jnp.float32
    nt = (((1,), (1,)), ((), ()))
    width = own.shape[0]
    half = width // 2
    pair = jnp.concatenate([own[...], one[...]], axis=0)
    strip[:width, :] = lax.dot_general(own[...], pair, nt, preferred_element_type=f32)
    block = lax.dot_general(one[...], three[...], nt, preferred_element_type=f32)
    strip[width:, :] = jnp.concatenate([block[:half], block[half:]], axis=1)


def gram_strip(own, one, three):
    width = own.shape[0]
    return pl.pallas_call(
        gram_kernel,
        out_shape=jax.ShapeDtypeStruct((width + width // 2, 2 * width), jnp.float32),
        in_specs=[vmem] * 3,
        out_specs=vmem,
        compiler_params=grant,
        name="gram_strip",
    )(own, one, three)


def three_parts(value):
    high = value.astype(jnp.bfloat16)
    rest = value - high.astype(jnp.float32)
    middle = rest.astype(jnp.bfloat16)
    low = (rest - middle.astype(jnp.float32)).astype(jnp.bfloat16)
    return high, middle, low


def solve_kernel(root, own_ref, *refs):
    strips, finals, rest = refs[:4], refs[4:8], refs[8:]
    far_basis, far_factor, basis, factor, work, inverse, sems = rest
    own = own_ref[0]
    n = work.shape[0]
    width = n // 4
    f32 = jnp.float32
    for k in range(4):
        source = lax.rem(own + 4 - k, 4)
        for part in range(4):

            @pl.when(source == part)
            def _(part=part, strip=strips[k]):
                spans = [slice(p * width, (p + 1) * width) for p in range(4)]
                here, back, ahead = spans[part], spans[part - 1], spans[(part + 1) % 4]
                work[here, here] = strip[:width, :width]
                if part == 0:
                    work[here, back] = strip[:width, width:]
                else:
                    work[back, here] = strip[:width, width:].T
                if part in (1, 2):
                    tail = strip[width:, :]
                    work[back, ahead] = jnp.concatenate([tail[:, :width], tail[:, width:]], axis=0)

    row_ids = lax.broadcasted_iota(jnp.int32, (PANEL, 128), 0)
    lane_ids = lax.broadcasted_iota(jnp.int32, (PANEL, 128), 1)
    rows = work[:PANEL, :]
    for r0 in range(0, n, PANEL):
        r1 = r0 + PANEL
        at, tile = r0 % 128, r0 // 128
        pivots = [
            jnp.broadcast_to(rows[:, r0 + k : r0 + k + 1], (PANEL, 128)) for k in range(PANEL)
        ]
        parts = [rows[:, t : t + 128] for t in range(0, n, 128)]
        parts.append(jnp.where(lane_ids - at == row_ids, 1.0, 0.0).astype(f32))
        diagonal = jnp.ones((PANEL, 128), f32)
        for j in range(PANEL):
            pivot = pivots[j][j : j + 1, :]
            diagonal = jnp.where(row_ids == j, pivot, diagonal)
            factors = jnp.where(row_ids > j, pivots[j] * (1.0 / pivot), 0.0)
            for k in range(j + 1, PANEL):
                pivots[k] = pivots[k] - factors * pivots[k][j : j + 1, :]
            parts = [q - factors * q[j : j + 1, :] for q in parts]
        roots = lax.rsqrt(diagonal)
        parts = [q * roots for q in parts]
        in_panel = (lane_ids >= at) & (lane_ids < at + PANEL)
        joined = []
        for t in range(n // 128):
            cols = lane_ids + 128 * t
            span = slice(128 * t, 128 * t + 128)
            factor[r0:r1, span] = jnp.where(cols >= row_ids + r0, parts[t] * (1.0 / root), 0.0)
            both = jnp.where(in_panel, parts[-1], parts[t]) if t == tile else parts[t]
            joined.append(both)
            inverse[r0:r1, span] = jnp.where(cols < r1, both, 0.0)
        if r1 < n:
            h, m, l = three_parts(jnp.concatenate(joined, axis=1))
            left = jnp.concatenate([h, h, m, m, h, l], axis=0)
            right = jnp.concatenate([h, m, h, m, l, h], axis=0)
            low = r1 // 128 * 128
            turned = left[:, low:].T
            for top, end in ((r1, r1 + PANEL), (r1 + PANEL, n)):
                if top < end:
                    span = slice(top - low, end - low)
                    update = jnp.dot(turned[span], right, preferred_element_type=f32)
                    cols = lax.broadcasted_iota(jnp.int32, (end - top, n), 1)
                    kept = jnp.where((cols >= r0) & (cols < r1), 0.0, work[top:end, :])
                    if top == r1:
                        rows = kept - update
                    else:
                        work[top:end, :] = kept - update
    copies = [pltpu.make_async_copy(factor, far_factor, sems.at[0])]
    copies[0].start()
    mine = root * inverse[pl.ds(pl.multiple_of(own * width, width), width), :]
    blocks = [mine[:, b * width : (b + 1) * width] for b in range(4)]
    ordered = []
    for k in range(4):
        source = lax.rem(own + 4 - k, 4)
        block = blocks[0]
        for b in range(1, 4):
            block = jnp.where(source == b, blocks[b], block)
        ordered.append(block)
    ordered = jnp.concatenate(ordered, axis=1)
    left = jnp.concatenate(three_parts(ordered), axis=0)
    wide = basis.shape[1] // PIECES
    for piece in range(PIECES):
        at = slice(piece * wide, (piece + 1) * wide)
        right = jnp.concatenate([f[:, at] for f in finals], axis=0)
        product = jnp.dot(left, right, preferred_element_type=f32)
        basis[:, at] = product[:width] + product[width : 2 * width] + product[2 * width :]
        span = pl.ds(piece * wide, wide)
        copy = pltpu.make_async_copy(
            basis.at[:, span], far_basis.at[:, span], sems.at[1 + piece]
        )
        copy.start()
        copies.append(copy)
    for copy in copies:
        copy.wait()


def solve(root, own, strips, finals):
    n = 2 * strips[0].shape[1]
    hbm = pl.BlockSpec(memory_space=pltpu.HBM)
    return pl.pallas_call(
        functools.partial(solve_kernel, root),
        out_shape=(
            jax.ShapeDtypeStruct(finals[0].shape, jnp.float32),
            jax.ShapeDtypeStruct((n, n), jnp.float32),
        ),
        in_specs=[smem] + [vmem] * 8,
        out_specs=(hbm,) * 2,
        scratch_shapes=[
            pltpu.VMEM(finals[0].shape, jnp.float32),
            pltpu.VMEM((n, n), jnp.float32),
            pltpu.VMEM((n, n), jnp.float32),
            pltpu.VMEM((n, n), jnp.float32),
            pltpu.SemaphoreType.DMA((1 + PIECES,)),
        ],
        compiler_params=grant,
        name="solve",
    )(own, *strips, *finals)


def shift(value, axis, by):
    n = lax.axis_size(axis)
    return lax.ppermute(value, axis, [(i, (i + by) % n) for i in range(n)])


def swap(value, axis, mask):
    n = lax.axis_size(axis)
    return lax.ppermute(value, axis, [(i, i ^ mask) for i in range(n)])


def xor_sum(value, axis, masks):
    terms = [value] + [swap(value, axis, m) for m in masks]
    while len(terms) > 1:
        terms = [terms[i] + terms[i + 1] for i in range(0, len(terms), 2)]
    return terms[0]


def far_away(value):
    return pltpu.with_memory_space_constraint(value, pltpu.HBM)


def body(subspace, onsite, blocks, cols):
    row_count = lax.axis_size("row")
    row_index = lax.axis_index("row")
    col_index = lax.axis_index("col").astype(jnp.int32)
    width, local_rows = subspace.shape
    slot_count, local_blocks, size, _ = blocks.shape
    at = jnp.stack([row_index.astype(jnp.int32), col_index])
    onsite = onsite[None, :]
    info, own, x, onsite, held, *send = send_part(row_count, at, cols.T, subspace, onsite, blocks)
    previous, before = None, x
    for step in range(FILTER):
        scale = filter_scale if step == 0 else 2.0 * filter_scale
        last = step == FILTER - 1
        keep = step < FILTER - 2
        halos = exchange(send, row_count)
        if step == 0:
            partial, table, held = first_part(
                scale, row_count, at, info, own, blocks, held, x, onsite
            )
        else:
            partial = local_part(scale, table, held, x, onsite, previous)
        x, *send = remote_part(scale, keep, last, table, halos, partial, x, held)
        previous = before
        if keep:
            before, *send = send
    final = x
    one = shift(final, "col", 1)
    three = shift(final, "col", -1)
    two = shift(one, "col", 1)
    strip = gram_strip(final, one, three)
    x_bit = row_count // 4
    strip = xor_sum(strip, "row", [1])
    strip = xor_sum(strip, "row", [2, 4, 6])
    strip = xor_sum(strip, "row", [x_bit, 2 * x_bit, 3 * x_bit])
    strips = [strip] + [shift(strip, "col", k) for k in (1, 2, 3)]
    root = math.sqrt(row_count * local_rows)
    return solve(root, at[1:], strips, [final, one, two, three])


def solution(mesh):
    in_specs = (P("col", "row"), P("row"), P(None, "row", None, None), P())
    out_specs = (P("col", "row"), P())
    return jax.shard_map(body, mesh=mesh, in_specs=in_specs, out_specs=out_specs, check_vma=False)
```

```python
import functools
import math

import jax
import jax.numpy as jnp
from jax import lax
from jax.experimental import pallas as pl
from jax.experimental.pallas import tpu as pltpu
from jax.sharding import PartitionSpec as P

HALO = 4
FILTER = 4
UNROLL = 16
LATE = 4
LOADS = 8
EARLY = 1
LANES = 128
COUNT = 32
SEND = 64
PANEL = 16
PIECES = 4

filter_scale = 0.4


def beside(here, row_count):
    odd = lax.rem(here, 2)
    return [here + 1 - 2 * odd, lax.rem(here + row_count - 1 + 2 * odd, row_count)]


def sources_of(here, row_count):
    ahead = [lax.rem(here + by, row_count) for by in (2, row_count // 2)]
    return beside(here, row_count) + ahead


def askers_of(here, row_count):
    behind = [lax.rem(here + row_count - by, row_count) for by in (2, row_count // 2)]
    return beside(here, row_count) + behind


def exchange(sends, row_count):
    devices = range(row_count)
    targets = [
        [i ^ 1 for i in devices],
        [(i + 1 if i % 2 else i - 1) % row_count for i in devices],
        [(i - 2) % row_count for i in devices],
        [(i - row_count // 2) % row_count for i in devices],
    ]
    return [
        lax.ppermute(send, "row", list(zip(devices, to))) for send, to in zip(sends, targets)
    ]


def spread(values, s, rows):
    return jnp.broadcast_to(values[:, s : s + 1], (rows, LANES))


def ranks_of(named, local_blocks):
    hits = jnp.max(named, axis=0, keepdims=True)
    above = lax.broadcasted_iota(jnp.int32, (LANES, LANES), 0)
    here = lax.broadcasted_iota(jnp.int32, (LANES, LANES), 1)
    before = (above < here) & (above // local_blocks == here // local_blocks)
    ranks = jnp.dot(
        jnp.broadcast_to(hits, (16, LANES)).astype(jnp.bfloat16),
        jnp.where(before, 1.0, 0.0).astype(jnp.bfloat16),
        preferred_element_type=jnp.float32,
    )
    return hits, ranks[:1]


def load(far, blocks, sem, g):
    slot_count, local_blocks, _, _ = blocks.shape
    share = local_blocks // LOADS
    for s in range(slot_count):
        part = pl.ds(g * share, share)
        pltpu.make_async_copy(far.at[s, part], blocks.at[s, part], sem).start()


def loaded(blocks, sem, g):
    share = blocks.shape[1] // LOADS
    part = blocks.at[:, pl.ds(g * share, share)]
    pltpu.make_async_copy(part, part, sem).wait()


def send_kernel(row_count, far_cols, far_x, far_onsite, far, *refs):
    info, own, x, onsite, blocks, *sends, cols, turned, sems = refs
    slot_count = cols.shape[0]
    _, local_blocks, size, _ = blocks.shape
    here = lax.axis_index("row")
    copies = [
        pltpu.make_async_copy(far_cols, cols, sems.at[0]),
        pltpu.make_async_copy(far_x, x, sems.at[1]),
        pltpu.make_async_copy(far_onsite, onsite, sems.at[2]),
    ]
    for copy in copies:
        copy.start()
    for g in range(EARLY):
        load(far, blocks, sems.at[3 + g], g)
    copies[0].wait()
    per_tile = LANES // local_blocks

    def rows_of(device):
        start = pl.multiple_of(device // per_tile * LANES, LANES)
        tile = cols[:, pl.ds(start, LANES)]
        pad = jnp.zeros((-slot_count % 8, LANES), jnp.int32)
        turned[:, : slot_count + pad.shape[0]] = jnp.concatenate([tile, pad], axis=0).T
        start = pl.multiple_of(lax.rem(device, per_tile) * local_blocks, local_blocks)
        return turned[pl.ds(start, local_blocks), :]

    lane = lax.broadcasted_iota(jnp.int32, (local_blocks, LANES), 1)
    named = jnp.zeros((local_blocks, LANES), jnp.float32)
    for q, asker in enumerate(askers_of(here, row_count)):
        values = rows_of(asker) - (here - q) * local_blocks
        group = lane // local_blocks == q
        for s in range(slot_count):
            named = jnp.where(group & (spread(values, s, local_blocks) == lane), 1.0, named)
    own[...] = rows_of(here)
    hits, ranks = ranks_of(named, local_blocks)
    entry = lax.broadcasted_iota(jnp.int32, (4 * HALO, LANES), 0)
    lane = lax.broadcasted_iota(jnp.int32, (4 * HALO, LANES), 1)
    chosen = (hits > 0) & (lane // local_blocks == entry // HALO)
    chosen = chosen & (ranks.astype(jnp.int32) == entry % HALO)
    numbers = jnp.where(chosen, (lane % local_blocks).astype(jnp.float32), 0.0)
    numbers = jnp.sum(numbers, axis=1, keepdims=True).astype(jnp.int32)
    for copy in copies[1:]:
        copy.wait()
    for q in range(4):
        for k in range(HALO):
            j = numbers[q * HALO + k, 0]
            info[q * HALO + k] = j
            sends[q][k] = x[:, pl.ds(pl.multiple_of(j * size, size), size)]
    for g in range(EARLY):
        loaded(blocks, sems.at[3 + g], g)


def send_part(row_count, cols, x, onsite, blocks):
    _, local_blocks, size, _ = blocks.shape
    send = jax.ShapeDtypeStruct((HALO, x.shape[0], size), jnp.bfloat16)
    whole = [jax.ShapeDtypeStruct(v.shape, v.dtype) for v in (x, onsite, blocks)]
    hbm = pl.BlockSpec(memory_space=pltpu.HBM)
    return pl.pallas_call(
        functools.partial(send_kernel, row_count),
        out_shape=(
            jax.ShapeDtypeStruct((4 * HALO,), jnp.int32),
            jax.ShapeDtypeStruct((local_blocks, LANES), jnp.int32),
            *whole,
        )
        + (send,) * 4,
        in_specs=[hbm] * 4,
        out_specs=(smem,) + (vmem,) * 8,
        scratch_shapes=[
            pltpu.VMEM(cols.shape, jnp.int32),
            pltpu.VMEM((LANES, LANES), jnp.int32),
            pltpu.SemaphoreType.DMA((3 + EARLY,)),
        ],
        compiler_params=grant,
        name="send_part",
    )(*[far_away(v) for v in (cols, x, onsite, blocks)])


def build_table(row_count, here, slot_count, values, info):
    rows = values.shape[0]
    lane = lax.broadcasted_iota(jnp.int32, (rows, LANES), 1)
    ids = jnp.zeros((rows, LANES), jnp.int32)
    for q, source in enumerate(sources_of(here, row_count)):
        ids = jnp.where(lane // rows == q, (source - q) * rows + lane, ids)
    columns = [spread(values, s, rows) for s in range(slot_count)]
    named = jnp.zeros((rows, LANES), jnp.float32)
    near_total = jnp.zeros((rows, LANES), jnp.int32)
    nears = []
    for column in columns:
        named = jnp.where(column == ids, 1.0, named)
        within = column - here * rows
        nears.append((within >= 0) & (within < rows))
        near_total = near_total + nears[-1].astype(jnp.int32)
    _, ranks = ranks_of(named, rows)
    group = lane[:1] // rows
    places = ranks + (HALO * group + rows + 1).astype(jnp.float32)
    near_count = jnp.zeros((rows, LANES), jnp.int32)
    table = jnp.zeros((rows, LANES), jnp.int32)
    for s, (column, near) in enumerate(zip(columns, nears)):
        far = jnp.sum(jnp.where(column == ids, places, 0.0), axis=1, keepdims=True)
        place = jnp.where(near, column - here * rows, far.astype(jnp.int32))
        rank = jnp.where(near, near_count, near_total + s - near_count)
        near_count = near_count + near.astype(jnp.int32)
        table = jnp.where(lane == rank, s * 64 + place, table)
    extra = (lane < slot_count - LATE) & ((table & 63) > rows)
    count = jnp.sum(extra.astype(jnp.float32)).astype(jnp.int32)
    table = jnp.where(lane == COUNT, count, table)
    for k in range(4 * HALO):
        table = jnp.where(lane == SEND + k, info[k], table)
    return table


def slot_pairs(table, row, slots, held, blocks, limit):
    total = None
    for t in range(slots.start, slots.stop, 2):
        codes = [table[row, t + k] for k in range(2)]
        places = [jnp.minimum(code & 63, limit) for code in codes]
        taken = jnp.concatenate([held[p] for p in places], axis=1)
        block = jnp.concatenate([blocks[code >> 6, row] for code in codes], axis=0)
        product = jnp.dot(taken, block, preferred_element_type=jnp.float32)
        total = product if total is None else total + product
    return total


def local_rows_of(scale, table, groups, unroll, blocks, onsite, prev, y, held):
    slot_count, local_blocks, size, _ = blocks.shape

    @pl.loop(groups[0], groups[1])
    def _(group):
        for u in range(unroll):
            row = group * unroll + u
            early = range(slot_count - LATE)
            total = slot_pairs(table, row, early, held, blocks, local_blocks)
            span = pl.ds(pl.multiple_of(row * size, size), size)
            value = scale * (total + onsite[:, span] * held[row].astype(jnp.float32))
            if prev is not None:
                value = value - prev[:, span].astype(jnp.float32)
            y[:, span] = value


def hold(x, held, local_blocks):
    size = held.shape[2]
    for j in range(local_blocks):
        held[j] = x[:, j * size : (j + 1) * size]
    held[local_blocks] = jnp.zeros(held.shape[1:], held.dtype)


def local_kernel(scale, table, blocks, x, onsite, prev, y, held):
    local_blocks = blocks.shape[1]
    hold(x, held, local_blocks)
    groups = (0, local_blocks // UNROLL)
    local_rows_of(scale, table, groups, UNROLL, blocks, onsite, prev, y, held)


def first_kernel(scale, row_count, info, own, far, started, x, onsite, *refs):
    y, table, blocks, held, near, sems = refs
    slot_count, local_blocks, _, _ = blocks.shape
    share = local_blocks // LOADS
    for g in range(EARLY, LOADS):
        load(far, blocks, sems.at[g], g)
    table[...] = build_table(row_count, lax.axis_index("row"), slot_count, own[...], info)
    copy = pltpu.make_async_copy(table, near, sems.at[LOADS])
    copy.start()
    hold(x, held, local_blocks)
    copy.wait()
    for g in range(LOADS):
        if g >= EARLY:
            loaded(blocks, sems.at[g], g)
        groups = (g, g + 1)
        local_rows_of(scale, near, groups, share, blocks, onsite, None, y, held)


def remote_kernel(scale, keep, last, table, *refs):
    halos, (y_in, x_in, blocks, x), rest = refs[:4], refs[4:8], refs[8:]
    y, sends, held = (rest[0], rest[1:-1], rest[-1]) if keep else (rest[-1], rest[:-2], rest[-2])
    slot_count, local_blocks, size, _ = blocks.shape
    per = halos[0].shape[0]
    count = table[0, COUNT]
    hold(x_in, held, local_blocks)
    for q in range(4):
        at = local_blocks + 1 + q * per
        held[at : at + per] = halos[q][...]

    @pl.loop(0, local_blocks // UNROLL)
    def _(group):
        for u in range(UNROLL):
            row = group * UNROLL + u
            late = range(slot_count - LATE, slot_count)
            total = slot_pairs(table, row, late, held, blocks, held.shape[0] - 1)
            span = pl.ds(pl.multiple_of(row * size, size), size)
            value = y_in[:, span] + scale * total
            y[:, span] = value
            x[:, span] = value.astype(jnp.bfloat16)

    @pl.when(count > 0)
    def _():
        @pl.loop(0, local_blocks)
        def _(row):
            @pl.loop(0, slot_count - LATE)
            def _(t):
                code = table[row, t]

                @pl.when((code & 63) > local_blocks)
                def _():
                    product = jnp.dot(
                        held[code & 63], blocks[code >> 6, row], preferred_element_type=jnp.float32
                    )
                    span = pl.ds(pl.multiple_of(row * size, size), size)
                    y[:, span] = y[:, span] + scale * product

        x[...] = y[...].astype(jnp.bfloat16)

    if not last:
        for q in range(4):
            for k in range(per):
                j = table[0, SEND + q * per + k]
                sends[q][k] = x[:, pl.ds(pl.multiple_of(j * size, size), size)]


vmem = pl.BlockSpec(memory_space=pltpu.VMEM)
smem = pl.BlockSpec(memory_space=pltpu.SMEM)
grant = pltpu.CompilerParams(vmem_limit_bytes=16 << 20)


def local_part(scale, table, blocks, x, onsite, prev):
    _, local_blocks, size, _ = blocks.shape
    return pl.pallas_call(
        functools.partial(local_kernel, scale),
        out_shape=jax.ShapeDtypeStruct(x.shape, jnp.float32),
        in_specs=[smem] + [vmem] * 4,
        out_specs=vmem,
        scratch_shapes=[pltpu.VMEM((local_blocks + 1, x.shape[0], size), jnp.bfloat16)],
        compiler_params=grant,
        name="local_part",
    )(table, blocks, x, onsite, prev)


def first_part(scale, row_count, info, own, far, started, x, onsite):
    _, local_blocks, size, _ = far.shape
    table = (local_blocks, LANES)
    hbm = pl.BlockSpec(memory_space=pltpu.HBM)
    return pl.pallas_call(
        functools.partial(first_kernel, scale, row_count),
        out_shape=(
            jax.ShapeDtypeStruct(x.shape, jnp.float32),
            jax.ShapeDtypeStruct(table, jnp.int32),
            jax.ShapeDtypeStruct(far.shape, far.dtype),
        ),
        in_specs=[smem, vmem, hbm, vmem, vmem, vmem],
        out_specs=(vmem,) * 3,
        scratch_shapes=[
            pltpu.VMEM((local_blocks + 1, x.shape[0], size), jnp.bfloat16),
            pltpu.SMEM(table, jnp.int32),
            pltpu.SemaphoreType.DMA((LOADS + 1,)),
        ],
        input_output_aliases={3: 2},
        compiler_params=grant,
        name="first_part",
    )(info, own, far, started, x, onsite)


def remote_part(scale, keep, last, table, halos, y, x, blocks):
    _, local_blocks, size, _ = blocks.shape
    width = y.shape[0]
    per = halos[0].shape[0]
    sends = () if last else (jax.ShapeDtypeStruct((per, width, size), jnp.bfloat16),) * 4
    kept = (jax.ShapeDtypeStruct(y.shape, jnp.float32),) if keep else ()
    scratch = [pltpu.VMEM((local_blocks + 1 + 4 * per, width, size), jnp.bfloat16)]
    if not keep:
        scratch.append(pltpu.VMEM(y.shape, jnp.float32))
    return pl.pallas_call(
        functools.partial(remote_kernel, scale, keep, last),
        out_shape=(jax.ShapeDtypeStruct(y.shape, jnp.bfloat16),) + kept + sends,
        in_specs=[smem] + [vmem] * 7,
        out_specs=(vmem,) * (1 + len(kept) + len(sends)),
        scratch_shapes=scratch,
        compiler_params=grant,
        name="remote_part",
    )(table, *halos, y, x, blocks)


def gram_kernel(own, one, three, strip):
    f32 = jnp.float32
    nt = (((1,), (1,)), ((), ()))
    width = own.shape[0]
    half = width // 2
    pair = jnp.concatenate([own[...], one[...]], axis=0)
    strip[:width, :] = lax.dot_general(own[...], pair, nt, preferred_element_type=f32)
    block = lax.dot_general(one[...], three[...], nt, preferred_element_type=f32)
    strip[width:, :] = jnp.concatenate([block[:half], block[half:]], axis=1)


def gram_strip(own, one, three):
    width = own.shape[0]
    return pl.pallas_call(
        gram_kernel,
        out_shape=jax.ShapeDtypeStruct((width + width // 2, 2 * width), jnp.float32),
        in_specs=[vmem] * 3,
        out_specs=vmem,
        compiler_params=grant,
        name="gram_strip",
    )(own, one, three)


def three_parts(value):
    high = value.astype(jnp.bfloat16)
    rest = value - high.astype(jnp.float32)
    middle = rest.astype(jnp.bfloat16)
    low = (rest - middle.astype(jnp.float32)).astype(jnp.bfloat16)
    return high, middle, low


def solve_kernel(root, *refs):
    strips, finals, rest = refs[:4], refs[4:8], refs[8:]
    far_basis, far_factor, basis, factor, work, inverse, sems = rest
    own = lax.axis_index("col")
    n = work.shape[0]
    width = n // 4
    f32 = jnp.float32
    for k in range(4):
        source = lax.rem(own + 4 - k, 4)
        for part in range(4):

            @pl.when(source == part)
            def _(part=part, strip=strips[k]):
                spans = [slice(p * width, (p + 1) * width) for p in range(4)]
                here, back, ahead = spans[part], spans[part - 1], spans[(part + 1) % 4]
                work[here, here] = strip[:width, :width]
                if part == 0:
                    work[here, back] = strip[:width, width:]
                else:
                    work[back, here] = strip[:width, width:].T
                if part in (1, 2):
                    tail = strip[width:, :]
                    work[back, ahead] = jnp.concatenate([tail[:, :width], tail[:, width:]], axis=0)

    row_ids = lax.broadcasted_iota(jnp.int32, (PANEL, 128), 0)
    lane_ids = lax.broadcasted_iota(jnp.int32, (PANEL, 128), 1)
    rows = work[:PANEL, :]
    for r0 in range(0, n, PANEL):
        r1 = r0 + PANEL
        at, tile = r0 % 128, r0 // 128
        pivots = [
            jnp.broadcast_to(rows[:, r0 + k : r0 + k + 1], (PANEL, 128)) for k in range(PANEL)
        ]
        parts = [rows[:, t : t + 128] for t in range(0, n, 128)]
        parts.append(jnp.where(lane_ids - at == row_ids, 1.0, 0.0).astype(f32))
        diagonal = jnp.ones((PANEL, 128), f32)
        for j in range(PANEL):
            pivot = pivots[j][j : j + 1, :]
            diagonal = jnp.where(row_ids == j, pivot, diagonal)
            factors = jnp.where(row_ids > j, pivots[j] * (1.0 / pivot), 0.0)
            for k in range(j + 1, PANEL):
                pivots[k] = pivots[k] - factors * pivots[k][j : j + 1, :]
            parts = [q - factors * q[j : j + 1, :] for q in parts]
        roots = lax.rsqrt(diagonal)
        parts = [q * roots for q in parts]
        in_panel = (lane_ids >= at) & (lane_ids < at + PANEL)
        joined = []
        for t in range(n // 128):
            cols = lane_ids + 128 * t
            span = slice(128 * t, 128 * t + 128)
            factor[r0:r1, span] = jnp.where(cols >= row_ids + r0, parts[t] * (1.0 / root), 0.0)
            both = jnp.where(in_panel, parts[-1], parts[t]) if t == tile else parts[t]
            joined.append(both)
            inverse[r0:r1, span] = jnp.where(cols < r1, both, 0.0)
        if r1 < n:
            h, m, l = three_parts(jnp.concatenate(joined, axis=1))
            left = jnp.concatenate([h, h, m, m, h, l], axis=0)
            right = jnp.concatenate([h, m, h, m, l, h], axis=0)
            low = r1 // 128 * 128
            turned = left[:, low:].T
            for top, end in ((r1, r1 + PANEL), (r1 + PANEL, n)):
                if top < end:
                    span = slice(top - low, end - low)
                    update = jnp.dot(turned[span], right, preferred_element_type=f32)
                    cols = lax.broadcasted_iota(jnp.int32, (end - top, n), 1)
                    kept = jnp.where((cols >= r0) & (cols < r1), 0.0, work[top:end, :])
                    if top == r1:
                        rows = kept - update
                    else:
                        work[top:end, :] = kept - update
    copies = [pltpu.make_async_copy(factor, far_factor, sems.at[0])]
    copies[0].start()
    mine = root * inverse[pl.ds(pl.multiple_of(own * width, width), width), :]
    blocks = [mine[:, b * width : (b + 1) * width] for b in range(4)]
    ordered = []
    for k in range(4):
        source = lax.rem(own + 4 - k, 4)
        block = blocks[0]
        for b in range(1, 4):
            block = jnp.where(source == b, blocks[b], block)
        ordered.append(block)
    ordered = jnp.concatenate(ordered, axis=1)
    left = jnp.concatenate(three_parts(ordered), axis=0)
    wide = basis.shape[1] // PIECES
    for piece in range(PIECES):
        at = slice(piece * wide, (piece + 1) * wide)
        right = jnp.concatenate([f[:, at] for f in finals], axis=0)
        product = jnp.dot(left, right, preferred_element_type=f32)
        basis[:, at] = product[:width] + product[width : 2 * width] + product[2 * width :]
        span = pl.ds(piece * wide, wide)
        copy = pltpu.make_async_copy(
            basis.at[:, span], far_basis.at[:, span], sems.at[1 + piece]
        )
        copy.start()
        copies.append(copy)
    for copy in copies:
        copy.wait()


def solve(root, strips, finals):
    n = 2 * strips[0].shape[1]
    hbm = pl.BlockSpec(memory_space=pltpu.HBM)
    return pl.pallas_call(
        functools.partial(solve_kernel, root),
        out_shape=(
            jax.ShapeDtypeStruct(finals[0].shape, jnp.float32),
            jax.ShapeDtypeStruct((n, n), jnp.float32),
        ),
        in_specs=[vmem] * 8,
        out_specs=(hbm,) * 2,
        scratch_shapes=[
            pltpu.VMEM(finals[0].shape, jnp.float32),
            pltpu.VMEM((n, n), jnp.float32),
            pltpu.VMEM((n, n), jnp.float32),
            pltpu.VMEM((n, n), jnp.float32),
            pltpu.SemaphoreType.DMA((1 + PIECES,)),
        ],
        compiler_params=grant,
        name="solve",
    )(*strips, *finals)


def shift(value, axis, by):
    n = lax.axis_size(axis)
    return lax.ppermute(value, axis, [(i, (i + by) % n) for i in range(n)])


def swap(value, axis, mask):
    n = lax.axis_size(axis)
    return lax.ppermute(value, axis, [(i, i ^ mask) for i in range(n)])


def xor_sum(value, axis, masks):
    terms = [value] + [swap(value, axis, m) for m in masks]
    while len(terms) > 1:
        terms = [terms[i] + terms[i + 1] for i in range(0, len(terms), 2)]
    return terms[0]


def far_away(value):
    return pltpu.with_memory_space_constraint(value, pltpu.HBM)


def body(subspace, onsite, blocks, cols):
    row_count = lax.axis_size("row")
    width, local_rows = subspace.shape
    slot_count, local_blocks, size, _ = blocks.shape
    onsite = onsite[None, :]
    info, own, x, onsite, held, *send = send_part(row_count, cols.T, subspace, onsite, blocks)
    previous, before = None, x
    for step in range(FILTER):
        scale = filter_scale if step == 0 else 2.0 * filter_scale
        last = step == FILTER - 1
        keep = step < FILTER - 2
        halos = exchange(send, row_count)
        if step == 0:
            partial, table, held = first_part(
                scale, row_count, info, own, blocks, held, x, onsite
            )
        else:
            partial = local_part(scale, table, held, x, onsite, previous)
        x, *send = remote_part(scale, keep, last, table, halos, partial, x, held)
        previous = before
        if keep:
            before, *send = send
    final = x
    one = shift(final, "col", 1)
    three = shift(final, "col", -1)
    two = shift(one, "col", 1)
    strip = gram_strip(final, one, three)
    x_bit = row_count // 4
    strip = xor_sum(strip, "row", [1])
    strip = xor_sum(strip, "row", [2, 4, 6])
    strip = xor_sum(strip, "row", [x_bit, 2 * x_bit, 3 * x_bit])
    strips = [strip] + [shift(strip, "col", k) for k in (1, 2, 3)]
    root = math.sqrt(row_count * local_rows)
    return solve(root, strips, [final, one, two, three])


def solution(mesh):
    in_specs = (P("col", "row"), P("row"), P(None, "row", None, None), P())
    out_specs = (P("col", "row"), P())
    return jax.shard_map(body, mesh=mesh, in_specs=in_specs, out_specs=out_specs, check_vma=False)
```
